128 devices in a mesh: ctx: 32 (over y, z, core), head: 4 (over x).
Axes of the slice: x: 4, y: 4, z: 4, core: 2. Of those that a mesh axis runs over, the one named last changes fastest.
Arguments:
- q_rows: bfloat16 [8192, 2048], P(('ctx', 'head')), may hold values from -6 to 6
- k_rows: bfloat16 [8192, 2048], P(('ctx', 'head')), may hold values from -6 to 6
- v_rows: bfloat16 [8192, 4096], P(('ctx', 'head')), may hold values from -6 to 6
- z_rows: bfloat16 [8192, 4096], P(('ctx', 'head')), may hold values from -6 to 6
- a_rows: bfloat16 [8192, 32], P(('ctx', 'head')), may hold values from -5 to 5
- b_rows: bfloat16 [8192, 32], P(('ctx', 'head')), may hold values from -11 to 5
- conv_q: float32 [4, 2048], P(None, 'head'), may hold values from -3 to 3
- conv_k: float32 [4, 2048], P(None, 'head'), may hold values from -3 to 3
- conv_v: float32 [4, 4096], P(None, 'head'), may hold values from -3 to 3
- a_log: float32 [32], P('head'), may hold values from -11 to -1
- dt_bias: float32 [32], P('head'), may hold values from -2 to 1
- norm_gain: float32 [128], replicated, may hold values from 0.5 to 1.5
Outputs:
- gated_out: bfloat16 [8192, 4096], P(('ctx', 'head'))
The draws below stay inside these ranges and needn't reach their ends.
All inputs are finite; a program needn't handle non-finite values.
Results may differ from the reference program's by a relative error of at most 0.0075.
Values may be sent and summed in bfloat16 or wider, within the bound.
A program may use at most 128 MiB of HBM per device.

```python
import jax
import jax.numpy as jnp
from jax import lax

KH = 16
VH = 32
DK = 128
DV = 128
CONV = 4
SPAN = 64
TOKENS = 8192


def draw_b_rows(key, part):
    level_key, noise_key = jax.random.split(jax.random.fold_in(key, 7))
    levels = jax.random.uniform(level_key, (VH,), jnp.float32, -7.0, 1.0)
    noise = jnp.clip(jax.random.normal(noise_key, (TOKENS, VH), jnp.float32), -4.0, 4.0)
    return (levels[None, :] + noise).astype(jnp.bfloat16)


def block_scale(own_key, shape, cuts, smallest, top_value):
    loudness, own = 1.0, jax.random.fold_in(own_key, 6)
    for dim, parts in cuts:
        heights = jnp.exp(jax.random.uniform(jax.random.fold_in(own, dim), (parts,), jnp.float32, smallest / len(cuts), top_value / len(cuts)))
        loudness = loudness * jnp.repeat(heights, shape[dim] // parts).reshape([-1 if axis == dim else 1 for axis in range(len(shape))])
    return loudness


def gaussian(stream_key, dims, deviation, limit, cuts=(), kind=jnp.bfloat16):
    entries = jax.random.normal(stream_key, dims, jnp.float32) * deviation
    if len(cuts) > 0:
        entries = block_scale(stream_key, dims, cuts, -0.22, 0.18) * entries
    return jnp.clip(entries, min=-limit, max=limit).astype(kind)


def setup_inputs(seed: int = 0) -> dict:
    key_of = jax.random.split(jax.random.key(seed), 13)
    return {
        "q_rows": gaussian(key_of[0], (TOKENS, KH * DK), 1.0, 6.0, ((0, 128),)),
        "k_rows": gaussian(key_of[1], (TOKENS, KH * DK), 1.0, 6.0, ((0, 128),)),
        "v_rows": gaussian(key_of[2], (TOKENS, VH * DV), 1.0, 6.0, ((0, 128),)),
        "z_rows": gaussian(key_of[3], (TOKENS, VH * DV), 1.0, 6.0, ((0, 128),)),
        "a_rows": gaussian(key_of[4], (TOKENS, VH), 1.0, 5.0, ((0, 128),)),
        "b_rows": draw_b_rows(jax.random.fold_in(key_of[12], 71), 0),
        "conv_q": gaussian(key_of[6], (CONV, KH * DK), 0.6, 3.0, ((1, 4),), jnp.float32),
        "conv_k": gaussian(key_of[7], (CONV, KH * DK), 0.6, 3.0, ((1, 4),), jnp.float32),
        "conv_v": gaussian(key_of[8], (CONV, VH * DV), 0.6, 3.0, ((1, 4),), jnp.float32),
        "a_log": jnp.clip(-11.0 + 10.0 * jax.random.uniform(key_of[9], (VH,), jnp.float32) ** block_scale(key_of[9], (VH,), ((0, 4),), -0.2, 0.2), -11.0, -1.0),
        "dt_bias": jnp.clip(-2.0 + 3.0 * jax.random.uniform(key_of[10], (VH,), jnp.float32) ** block_scale(key_of[10], (VH,), ((0, 4),), -0.2, 0.2), -2.0, 1.0),
        "norm_gain": jnp.clip(1.0 + 0.1 * jax.random.normal(key_of[11], (DV,), jnp.float32), 0.5, 1.5),
    }


HIGHEST = lax.Precision.HIGHEST

def conv_silu(seq_rows, rim_rows, weight):
    padded = jnp.concatenate([rim_rows, seq_rows], axis=0).astype(jnp.float32)
    length_rows = seq_rows.shape[0]
    summed = weight[0] * padded[0:length_rows]
    for offset in range(1, weight.shape[0]):
        summed = summed + weight[offset] * padded[offset:offset + length_rows]
    return jax.nn.silu(summed)

def unit_norm(conv_out, head_width, factor):
    shaped = conv_out.reshape(conv_out.shape[0], -1, head_width)
    scaled = shaped * lax.rsqrt(lax.optimization_barrier(jnp.sum(shaped * shaped, axis=-1, keepdims=True)) + 1e-06) * factor
    return scaled.astype(jnp.bfloat16)

def span_parts(q_block, k_block, v_block, g_block, b_block):
    length_rows = g_block.shape[1]
    cum_decay = jnp.cumsum(g_block, axis=1)
    row_ids = lax.broadcasted_iota(jnp.int32, (length_rows, length_rows), 0)
    col_ids = lax.broadcasted_iota(jnp.int32, (length_rows, length_rows), 1)
    lower_mask = row_ids >= col_ids
    gap_log = cum_decay[:, :, None] - cum_decay[:, None, :]
    within = jnp.where(lower_mask, jnp.exp(jnp.where(lower_mask, gap_log, 0.0)), 0.0)
    k_gram = jnp.einsum('hid,hjd->hij', k_block, k_block, precision=HIGHEST)
    strict_part = jnp.where(row_ids > col_ids, b_block[:, :, None] * within * k_gram, 0.0)
    system_mat = strict_part + jnp.eye(length_rows, dtype=jnp.float32)
    growth = jnp.exp(cum_decay)
    right_side = jnp.concatenate([(b_block * growth)[:, :, None] * k_block, b_block[:, :, None] * v_block], axis=2)
    solved = jax.scipy.linalg.solve_triangular(system_mat, right_side, lower=True, unit_diagonal=True)
    key_width = k_block.shape[2]
    w_mat = solved[:, :, :key_width]
    u_mat = solved[:, :, key_width:]
    scores = jnp.einsum('hid,hjd->hij', q_block, k_block, precision=HIGHEST) * within
    q_decay = growth[:, :, None] * q_block
    end_decay = growth[:, -1]
    k_decay = jnp.exp(cum_decay[:, -1:] - cum_decay)[:, :, None] * k_block
    return (q_decay, scores, w_mat, u_mat, k_decay, end_decay)

def reference(q_rows, k_rows, v_rows, z_rows, a_rows, b_rows, conv_q, conv_k, conv_v, a_log, dt_bias, norm_gain):
    rim_keys = jnp.zeros((CONV - 1, KH * DK), jnp.bfloat16)
    rim_vals = jnp.zeros((CONV - 1, VH * DV), jnp.bfloat16)
    queries = unit_norm(conv_silu(q_rows, rim_keys, conv_q), DK, DK ** (-0.5))
    keys_unit = unit_norm(conv_silu(k_rows, rim_keys, conv_k), DK, 1.0)
    values = conv_silu(v_rows, rim_vals, conv_v).astype(jnp.bfloat16).reshape(TOKENS, VH, DV)
    write_rate = jax.nn.sigmoid(b_rows.astype(jnp.float32))
    log_decay = -jnp.exp(a_log)[None, :] * jax.nn.softplus(a_rows.astype(jnp.float32) + dt_bias[None, :])
    span_count = TOKENS // SPAN
    q_all = queries.reshape(span_count, SPAN, KH, DK).transpose(0, 2, 1, 3)
    k_all = keys_unit.reshape(span_count, SPAN, KH, DK).transpose(0, 2, 1, 3)
    v_all = values.reshape(span_count, SPAN, VH, DV).transpose(0, 2, 1, 3)
    g_all = log_decay.reshape(span_count, SPAN, VH).transpose(0, 2, 1)
    b_all = write_rate.reshape(span_count, SPAN, VH).transpose(0, 2, 1)
    share_ratio = VH // KH

    def advance(state_now, pieces):
        q_block, k_block, v_block, g_block, b_block = pieces
        q_full = jnp.repeat(q_block.astype(jnp.float32), share_ratio, axis=0)
        k_full = jnp.repeat(k_block.astype(jnp.float32), share_ratio, axis=0)
        q_decay, scores, w_mat, u_mat, k_decay, end_decay = span_parts(q_full, k_full, v_block.astype(jnp.float32), g_block, b_block)
        fresh_vals = u_mat - jnp.einsum('hcd,hde->hce', w_mat, state_now, precision=HIGHEST)
        output = jnp.einsum('hcd,hde->hce', q_decay, state_now, precision=HIGHEST) + jnp.einsum('hij,hje->hie', scores, fresh_vals, precision=HIGHEST)
        state_next = end_decay[:, None, None] * state_now + jnp.einsum('hcd,hce->hde', k_decay, fresh_vals, precision=HIGHEST)
        return (state_next, output)
    state_first = jnp.zeros((VH, DK, DV), jnp.float32)
    _, outputs = lax.scan(advance, state_first, (q_all, k_all, v_all, g_all, b_all))
    core_out = outputs.transpose(0, 2, 1, 3).reshape(TOKENS, VH, DV)
    normed = (core_out * lax.rsqrt(lax.optimization_barrier(jnp.mean(core_out * core_out, axis=-1, keepdims=True)) + 1e-06) * norm_gain).astype(jnp.bfloat16)
    normed = lax.optimization_barrier(normed)
    gated_out = normed.astype(jnp.float32).reshape(TOKENS, VH * DV) * jax.nn.silu(z_rows.astype(jnp.float32))
    return gated_out.astype(jnp.bfloat16)
```

```python
import functools

import jax
import jax.numpy as jnp
from jax import lax
from jax.experimental import pallas as pl
from jax.experimental.pallas import tpu as pltpu
from jax.sharding import PartitionSpec as P

MESH = pl.DeviceIdType.MESH
F32 = jnp.float32
BF = jnp.bfloat16
HIGHEST = lax.Precision.HIGHEST

D = 128
BLK = 64
C = 256
HK = 4
HV = 8
NH = 4
GRP = 8
MAPR = 2 * D + 16


def nn(a, b, precision=None):
    return lax.dot_general(
        a, b, (((1,), (0,)), ((), ())), precision=precision, preferred_element_type=F32
    )


def nt(a, b):
    return lax.dot_general(a, b, (((1,), (1,)), ((), ())), preferred_element_type=F32)


def bdot(a, b):
    return nn(a.astype(BF), b.astype(BF))


def sigmoid(x):
    return 1.0 / (1.0 + jnp.exp(-x))


def remote(src, dst, send, recv, where):
    return pltpu.make_async_remote_copy(
        src_ref=src, dst_ref=dst, send_sem=send, recv_sem=recv, device_id=where, device_id_type=MESH
    )


def triangle_inverse(n_blk, row, col):
    size = n_blk.shape[0]
    diff = row ^ col
    t_mat = jnp.where(row == col, 1.0, jnp.where(diff == 1, -n_blk, 0.0))
    step = 2
    while step < size:
        tb = t_mat.astype(BF)
        off = jnp.where((diff >= step) & (diff < 2 * step), n_blk, 0.0).astype(BF)
        t_mat = t_mat - nn(nn(tb, off).astype(BF), tb)
        step *= 2
    return jnp.where(row == col, 0.0, t_mat)


def kernel(
    q, k, v, z, a, b, cq, ck, cv, alog, dtb, gain,
    out,
    rq, rk, rv, ra, rb, hq, hk, hv, zin, sz, xs,
    ccol, crow, pmat, xmat, qs, o0, gmat,
    msend, maps, pxd, pxa, pep, gsend, gmap, state, ssend, sbuf, nb, fo,
    a2a_s, a2a_r, ab_s, ab_r, halo_s, halo_r, loc, zsem, map_s, map_r, y_s, y_r, st_s, st_r, ret_s, ret_r,
):
    ctx = lax.axis_index("ctx")
    me = lax.axis_index("head")
    nctx = lax.axis_size("ctx")
    base = (ctx // GRP) * GRP
    mine = ctx - base
    yrow = ctx // GRP
    nrow = nctx // GRP
    prev = lax.rem(ctx + nctx - 1, nctx)
    nxt = lax.rem(ctx + 1, nctx)

    def peer(d):
        return lax.rem(me + d, NH)

    def source(d):
        return lax.rem(me + NH - d, NH)

    def own_copies():
        cps = []
        for i, (src, dst, w) in enumerate(((q, rq, 512), (k, rk, 512), (v, rv, 1024))):
            cps.append(
                pltpu.make_async_copy(
                    src.at[:, pl.ds(pl.multiple_of(me * w, w), w)],
                    dst.at[pl.ds(pl.multiple_of(me * BLK, BLK), BLK), :],
                    loc.at[i],
                )
            )
        for i, (src, dst) in enumerate(((a, ra), (b, rb))):
            cps.append(
                pltpu.make_async_copy(src, dst.at[pl.ds(pl.multiple_of(me * BLK, BLK), BLK), :], loc.at[3 + i])
            )
        return cps

    zcopy = pltpu.make_async_copy(z, zin, zsem)
    zcopy.start()
    for cp in own_copies():
        cp.start()

    barrier = pltpu.get_barrier_semaphore()
    for d in range(1, NH):
        pl.semaphore_signal(barrier, inc=1, device_id={"head": peer(d)}, device_id_type=MESH)
    for d in range(1, GRP):
        pl.semaphore_signal(barrier, inc=1, device_id={"ctx": base + lax.rem(mine + d, GRP)}, device_id_type=MESH)
    for d in range(1, 4):
        pl.semaphore_signal(barrier, inc=1, device_id={"ctx": lax.rem(ctx + d * GRP, nctx)}, device_id_type=MESH)

    @pl.when(me < NH - 1)
    def _():
        pl.semaphore_signal(barrier, inc=1, device_id={"ctx": prev, "head": NH - 1}, device_id_type=MESH)

    @pl.when(me == NH - 1)
    def _():
        pl.semaphore_signal(barrier, inc=1, device_id={"ctx": prev}, device_id_type=MESH)
        for p in range(NH - 1):
            pl.semaphore_signal(barrier, inc=1, device_id={"ctx": nxt, "head": p}, device_id_type=MESH)
        pl.semaphore_signal(barrier, inc=1, device_id={"ctx": nxt}, device_id_type=MESH)

    pl.semaphore_wait(barrier, jnp.where(me == NH - 1, 3 + 7 + 3 + 1 + 4, 3 + 7 + 3 + 1))

    def ab_copy(d, i):
        src, dst = ((a, ra), (b, rb))[i]
        return remote(
            src, dst.at[pl.ds(pl.multiple_of(me * BLK, BLK), BLK), :], ab_s.at[d - 1, i], ab_r.at[d - 1, i],
            {"head": peer(d)},
        )

    def rows_copy(d, kh, i):
        src, dst, w, cw = ((q, rq, 512, D), (k, rk, 512, D), (v, rv, 1024, 2 * D))[i]
        return remote(
            src.at[:, pl.ds(pl.multiple_of(peer(d) * w + kh * cw, cw), cw)],
            dst.at[pl.ds(pl.multiple_of(me * BLK, BLK), BLK), pl.ds(pl.multiple_of(kh * cw, cw), cw)],
            a2a_s.at[kh, d - 1, i], a2a_r.at[kh, d - 1, i], {"head": peer(d)},
        )

    def halo_copy(p, i):
        src, dst, w = ((q, hq, 512), (k, hk, 512), (v, hv, 1024))[i]
        where = {"ctx": nxt} if p == NH - 1 else {"ctx": nxt, "head": p}
        return remote(src.at[pl.ds(BLK - 16, 16), pl.ds(p * w, w)], dst, halo_s.at[p, i], halo_r.at[i], where)

    for d in (2, 1, 3):
        for i in range(2):
            ab_copy(d, i).start()

    @pl.when(me == NH - 1)
    def _():
        for p in range(NH):
            for i in range(3):
                halo_copy(p, i).start()

    @pl.loop(0, HK)
    def _(kh):
        for d in (2, 1, 3):
            for i in range(3):
                rows_copy(d, kh, i).start()

    zcopy.wait()

    @pl.loop(0, 8)
    def _(i):
        cols = pl.ds(pl.multiple_of(i * 512, 512), 512)
        zf = zin[:, cols].astype(F32)
        sz[:, cols] = zf * sigmoid(zf)

    for cp in own_copies():
        cp.wait()
    for d in range(1, NH):
        for i in range(2):
            ab_copy(d, i).wait_recv()
    sel = (
        lax.broadcasted_iota(jnp.int32, (32, HV), 0) == lax.broadcasted_iota(jnp.int32, (32, HV), 1) + me * HV
    ).astype(F32).astype(BF)
    sel_t = (
        lax.broadcasted_iota(jnp.int32, (HV, 32), 1) == lax.broadcasted_iota(jnp.int32, (HV, 32), 0) + me * HV
    ).astype(F32).astype(BF)
    eye8 = lax.broadcasted_iota(jnp.int32, (HV, HV), 0) == lax.broadcasted_iota(jnp.int32, (HV, HV), 1)

    def softplus(x):
        return jnp.maximum(x, 0.0) + jnp.log1p(jnp.exp(-jnp.abs(x)))

    def column(row):
        return jnp.sum(jnp.where(eye8, jnp.broadcast_to(row, (HV, HV)), 0.0), axis=1, keepdims=True)

    a_rows, b_rows = ra[...], rb[...]
    rate_row, bias_row = jnp.exp(alog[...]), dtb[...]
    g_col = -rate_row * softplus(nn(a_rows, sel) + bias_row)
    g_row = -column(rate_row) * softplus(nt(sel_t, a_rows) + column(bias_row))
    beta = sigmoid(nn(b_rows, sel))
    row = lax.broadcasted_iota(jnp.int32, (C, C), 0)
    col = lax.broadcasted_iota(jnp.int32, (C, C), 1)
    c_col = nn((row >= col).astype(F32), g_col, HIGHEST)
    c_row = nn(g_row, (row <= col).astype(F32), HIGHEST)
    for kh in range(HK):
        ccol[kh, :, 0:2] = c_col[:, 2 * kh : 2 * kh + 2]
        ccol[kh, :, 2:4] = beta[:, 2 * kh : 2 * kh + 2]
    for h in range(HV):
        crow[h] = c_row[h : h + 1, :]

    for i in range(3):
        halo_copy(0, i).wait_recv()
    inside = jnp.where(ctx > 0, 1.0, 0.0).astype(F32)

    def map_copy(m, slot):
        return remote(msend.at[m], maps.at[mine], map_s.at[m], map_r.at[slot], {"ctx": base + m})

    @pl.loop(0, HK)
    def _(kh):
        for d in range(1, NH):
            for i in range(3):
                rows_copy(d, kh, i).wait_recv()
        cols1 = pl.ds(pl.multiple_of(kh * D, D), D)
        cols2 = pl.ds(pl.multiple_of(kh * 2 * D, 2 * D), 2 * D)

        def conv_silu(rows, halo, taps, cols, width):
            xs[pl.ds(0, 16), pl.ds(0, width)] = halo[:, cols].astype(F32) * inside
            xs[pl.ds(16, C), pl.ds(0, width)] = rows[:, cols].astype(F32)
            w = taps[:, cols]
            total = w[0:1, :] * xs[pl.ds(13, C), pl.ds(0, width)]
            for j in range(1, 4):
                total = total + w[j : j + 1, :] * xs[pl.ds(13 + j, C), pl.ds(0, width)]
            return total * sigmoid(total)

        qc = conv_silu(rq, hq, cq, cols1, D)
        qn = (qc * lax.rsqrt(jnp.sum(qc * qc, axis=-1, keepdims=True) + 1e-6) * (D ** -0.5)).astype(BF)
        kc = conv_silu(rk, hk, ck, cols1, D)
        kn = (kc * lax.rsqrt(jnp.sum(kc * kc, axis=-1, keepdims=True) + 1e-6)).astype(BF)
        vn = conv_silu(rv, hv, cv, cols2, 2 * D).astype(BF).astype(F32)
        qs[kh] = qn
        kf = kn.astype(F32)
        kt = jnp.transpose(kf)
        kk = nt(kn, kn)
        qk = nt(qn, kn)
        cc = ccol[kh]
        r1 = lax.broadcasted_iota(jnp.int32, (D, D), 0)
        c1 = lax.broadcasted_iota(jnp.int32, (D, D), 1)
        rw = lax.broadcasted_iota(jnp.int32, (C, C), 0)
        cl = lax.broadcasted_iota(jnp.int32, (C, C), 1)
        for j in range(2):
            h = 2 * kh + j
            cj, bj = cc[:, j : j + 1], cc[:, 2 + j : 3 + j]
            cr = crow[h]
            within = jnp.where(rw >= cl, jnp.exp(jnp.minimum(cj - cr, 0.0)), 0.0)
            pmat[h] = (within * qk).astype(BF)
            n_mat = jnp.where(rw > cl, bj * within * kk, 0.0)
            grow = jnp.exp(cj)
            rhs = jnp.concatenate([bj * vn[:, j * D : (j + 1) * D], (bj * grow) * kf], axis=1)
            t0 = triangle_inverse(n_mat[:D, :D], r1, c1)
            t1 = triangle_inverse(n_mat[D:, D:], r1, c1)
            x0 = rhs[:D] + bdot(t0, rhs[:D])
            s1 = rhs[D:] - bdot(n_mat[D:, :D], x0)
            x1 = s1 + bdot(t1, s1)
            xb = jnp.concatenate([x0, x1], axis=0).astype(BF)
            xmat[h] = xb
            c_end = cr[:, C - 1 : C]
            kdt = (kt * jnp.exp(c_end - cr)).astype(BF)
            mm = nn(kdt, xb)
            msend[h, pl.ds(0, D), :] = (-mm[:, D:]).astype(BF)
            msend[h, pl.ds(D, D), :] = mm[:, :D].astype(BF)
            e_row = jnp.broadcast_to(jnp.exp(c_end), (16, D))
            e1 = e_row.astype(BF).astype(F32)
            e2 = (e_row - e1).astype(BF).astype(F32)
            e3 = e_row - e1 - e2
            ri = lax.broadcasted_iota(jnp.int32, (16, D), 0)
            parts = jnp.where(ri == 0, e1, jnp.where(ri == 1, e2, jnp.where(ri == 2, e3, 0.0)))
            msend[h, pl.ds(2 * D, 16), :] = parts.astype(BF)
        for j in range(2):
            h = 2 * kh + j

            @pl.when(h != mine)
            def _():
                map_copy(h, mine).start()

            @pl.when(h == mine)
            def _():
                pltpu.make_async_copy(msend.at[h], maps.at[mine], loc.at[5]).start()

    @pl.loop(0, HV)
    def _(h):
        px = nn(pmat[h], xmat[h])
        o0[h] = px[:, :D]
        gmat[h] = (jnp.exp(ccol_at(ccol, h)) * qs[h // 2].astype(F32) - px[:, D:]).astype(BF)

    def decay_of(ref, i):
        p = ref[i, pl.ds(2 * D, 16), :].astype(F32)
        return p[0:1, :] + p[1:2, :] + p[2:3, :]

    def wait_map(i):
        @pl.when(mine != i)
        def _():
            remote(msend.at[i], maps.at[i], map_s.at[i], map_r.at[i], {"ctx": base + i}).wait_recv()

        @pl.when(mine == i)
        def _():
            pltpu.make_async_copy(msend.at[i], maps.at[i], loc.at[5]).wait()

    wait_map(0)
    xd = maps[0, pl.ds(0, D), :].astype(F32)
    xa = maps[0, pl.ds(D, D), :].astype(F32)
    ep = decay_of(maps, 0)
    for i in range(1, GRP):
        pxd[i] = xd.astype(BF)
        pxa[i] = xa
        pep[i] = ep
        wait_map(i)
        lin = maps[i, pl.ds(0, D), :]
        e_i = decay_of(maps, i)
        both = nn(lin, jnp.concatenate([xd.astype(BF), xa.astype(BF)], axis=1))
        xd = e_i * xd + both[:, :D] + ep * lin.astype(F32)
        xa = e_i * xa + both[:, D:] + maps[i, pl.ds(D, D), :].astype(F32)
        ep = ep * e_i
    gsend[pl.ds(0, D), :] = xd.astype(BF)
    gsend[pl.ds(D, D), :] = xa.astype(BF)
    e1 = ep.astype(BF).astype(F32)
    e2 = (ep - e1).astype(BF).astype(F32)
    e3 = ep - e1 - e2
    ri = lax.broadcasted_iota(jnp.int32, (16, D), 0)
    gsend[pl.ds(2 * D, 16), :] = jnp.where(
        ri == 0, e1, jnp.where(ri == 1, e2, jnp.where(ri == 2, e3, 0.0))
    ).astype(BF)

    def row_copy(d):
        return remote(gsend, gmap.at[yrow], y_s.at[d - 1], y_r.at[yrow], {"ctx": lax.rem(ctx + d * GRP, nctx)})

    for d in range(1, 4):
        @pl.when(yrow + d < nrow)
        def _():
            row_copy(d).start()

    state[...] = jnp.zeros_like(state)
    for yy in range(3):
        @pl.when(yy < yrow)
        def _():
            remote(gsend, gmap.at[yy], y_s.at[0], y_r.at[yy], {"ctx": prev}).wait_recv()
            s_now = state[...]
            state[...] = (
                decay_of(gmap, yy) * s_now
                + nn(gmap[yy, pl.ds(0, D), :], s_now.astype(BF))
                + gmap[yy, pl.ds(D, D), :].astype(F32)
            )

    def state_copy(i, slot):
        return remote(ssend.at[i], sbuf.at[mine], st_s.at[i], st_r.at[slot], {"ctx": base + i})

    s_in = state[...]
    sb = s_in.astype(BF)
    for i in range(GRP):
        if i == 0:
            ssend[i] = sb
        else:
            ssend[i] = (pep[i] * s_in + nn(pxd[i], sb) + pxa[i]).astype(BF)

        @pl.when(mine != i)
        def _():
            state_copy(i, mine).start()

        @pl.when(mine == i)
        def _():
            pltpu.make_async_copy(ssend.at[i], sbuf.at[mine], loc.at[6]).start()

    def ret_copy(d, h, slot):
        return remote(
            nb.at[pl.ds(pl.multiple_of(peer(d) * BLK, BLK), BLK), pl.ds(pl.multiple_of(h * D, D), D)],
            fo.at[:, pl.ds(pl.multiple_of(me * HV * D + h * D, D), D)],
            ret_s.at[h, d - 1], ret_r.at[h, slot], {"head": peer(d)},
        )

    @pl.loop(0, HV)
    def _(h):
        @pl.when(h != mine)
        def _():
            remote(ssend.at[h], sbuf.at[h], st_s.at[h], st_r.at[h], {"ctx": base + h}).wait_recv()

        @pl.when(h == mine)
        def _():
            pltpu.make_async_copy(ssend.at[h], sbuf.at[h], loc.at[6]).wait()

        core = o0[h] + nn(gmat[h], sbuf[h])
        inv = lax.rsqrt(jnp.mean(core * core, axis=-1, keepdims=True) + 1e-6)
        nb[:, pl.ds(pl.multiple_of(h * D, D), D)] = (core * inv * gain[...]).astype(BF)
        for d in (2, 1, 3):
            ret_copy(d, h, d - 1).start()

    own = pltpu.make_async_copy(
        nb.at[pl.ds(pl.multiple_of(me * BLK, BLK), BLK), :],
        fo.at[:, pl.ds(pl.multiple_of(me * HV * D, HV * D), HV * D)],
        loc.at[7],
    )
    own.start()
    own.wait()

    def gate(src):
        @pl.loop(0, 2)
        def _(i):
            cols = pl.ds(pl.multiple_of(src * HV * D + i * 512, 512), 512)
            out[:, cols] = (fo[:, cols].astype(F32) * sz[:, cols]).astype(BF)

    gate(me)
    for d in (1, 3, 2):
        @pl.loop(0, HV)
        def _(h):
            ret_copy(d, h, d - 1).wait_recv()
        gate(source(d))

    for d in range(1, NH):
        for i in range(2):
            ab_copy(d, i).wait_send()
        @pl.loop(0, HK)
        def _(kh):
            for i in range(3):
                rows_copy(d, kh, i).wait_send()
        @pl.loop(0, HV)
        def _(h):
            ret_copy(d, h, d - 1).wait_send()
        @pl.when(yrow + d < nrow)
        def _():
            row_copy(d).wait_send()

    @pl.when(me == NH - 1)
    def _():
        for p in range(NH):
            for i in range(3):
                halo_copy(p, i).wait_send()

    @pl.loop(0, GRP)
    def _(i):
        @pl.when(i != mine)
        def _():
            map_copy(i, mine).wait_send()
            state_copy(i, mine).wait_send()


def ccol_at(ccol, h):
    kh, j = h // 2, h % 2
    pair = ccol[kh]
    return jnp.where(j == 0, pair[:, 0:1], pair[:, 1:2])


def local(q, k, v, z, a, b, cq, ck, cv, alog, dtb, gain):
    any_spec = pl.BlockSpec(memory_space=pl.ANY)
    vm = pl.BlockSpec(memory_space=pltpu.VMEM)
    dma = pltpu.SemaphoreType.DMA
    return pl.pallas_call(
        kernel,
        out_shape=jax.ShapeDtypeStruct((BLK, 4 * HV * D), BF),
        in_specs=[any_spec] * 6 + [vm] * 6,
        out_specs=vm,
        scratch_shapes=[
            pltpu.VMEM((C, 512), BF), pltpu.VMEM((C, 512), BF), pltpu.VMEM((C, 1024), BF),
            pltpu.VMEM((C, 32), BF), pltpu.VMEM((C, 32), BF),
            pltpu.VMEM((16, 512), BF), pltpu.VMEM((16, 512), BF), pltpu.VMEM((16, 1024), BF),
            pltpu.VMEM((BLK, 4096), BF), pltpu.VMEM((BLK, 4096), F32),
            pltpu.VMEM((C + 16, 256), F32),
            pltpu.VMEM((HK, C, 4), F32), pltpu.VMEM((HV, 1, C), F32),
            pltpu.VMEM((HV, C, C), BF), pltpu.VMEM((HV, C, C), BF), pltpu.VMEM((HK, C, D), BF),
            pltpu.VMEM((HV, C, D), F32), pltpu.VMEM((HV, C, D), BF),
            pltpu.VMEM((HV, MAPR, D), BF), pltpu.VMEM((GRP, MAPR, D), BF),
            pltpu.VMEM((GRP, D, D), BF), pltpu.VMEM((GRP, D, D), F32), pltpu.VMEM((GRP, 1, D), F32),
            pltpu.VMEM((MAPR, D), BF), pltpu.VMEM((4, MAPR, D), BF),
            pltpu.VMEM((D, D), F32), pltpu.VMEM((GRP, D, D), BF), pltpu.VMEM((HV, D, D), BF),
            pltpu.VMEM((C, HV * D), BF), pltpu.VMEM((BLK, 4 * HV * D), BF),
            dma((HK, 3, 3)), dma((HK, 3, 3)), dma((3, 2)), dma((3, 2)), dma((4, 3)), dma((3,)), dma((8,)), dma,
            dma((GRP,)), dma((GRP,)), dma((3,)), dma((4,)), dma((GRP,)), dma((GRP,)), dma((HV, 3)), dma((HV, 3)),
        ],
        compiler_params=pltpu.CompilerParams(
            collective_id=0, has_side_effects=True, vmem_limit_bytes=40 * 1024 * 1024
        ),
    )(q, k, v, z, a, b, cq, ck, cv, alog.reshape(1, HV), dtb.reshape(1, HV), gain.reshape(1, D))


def solution(mesh):
    rows = P(("ctx", "head"), None)
    placed = (rows,) * 6 + (P(None, "head"),) * 3 + (P("head"), P("head"), P())
    return jax.shard_map(local, mesh=mesh, in_specs=placed, out_specs=rows, check_vma=False)
```

```python
import functools

import jax
import jax.numpy as jnp
from jax import lax
from jax.experimental import pallas as pl
from jax.experimental.pallas import tpu as pltpu
from jax.sharding import PartitionSpec as P

MESH = pl.DeviceIdType.MESH
F32 = jnp.float32
BF = jnp.bfloat16
HIGHEST = lax.Precision.HIGHEST

D = 128
BLK = 64
C = 256
HK = 4
HV = 8
NH = 4
GRP = 8
RIM = 8
NEG = -1e30


def nn(a, b, precision=None):
    return lax.dot_general(
        a, b, (((1,), (0,)), ((), ())), precision=precision, preferred_element_type=F32
    )


def nt(a, b):
    return lax.dot_general(a, b, (((1,), (1,)), ((), ())), preferred_element_type=F32)


def sigmoid(x):
    return 1.0 / (1.0 + jnp.exp(-x))


def remote(src, dst, send, recv, where):
    return pltpu.make_async_remote_copy(
        src_ref=src, dst_ref=dst, send_sem=send, recv_sem=recv, device_id=where, device_id_type=MESH
    )


def aligned(x, n):
    return pl.multiple_of(x, n)


def store_exact(ref, row):
    wide = jnp.broadcast_to(row, (16, D))
    e1 = wide.astype(BF).astype(F32)
    e2 = (wide - e1).astype(BF).astype(F32)
    e3 = wide - e1 - e2
    i = lax.broadcasted_iota(jnp.int32, (16, D), 0)
    ref[pl.ds(D, 16), :] = jnp.where(i == 0, e1, jnp.where(i == 1, e2, jnp.where(i == 2, e3, 0.0))).astype(BF)


def load_exact(ref):
    p = ref[pl.ds(D, 16), :].astype(F32)
    return p[0:1, :] + p[1:2, :] + p[2:3, :]


def times_inverse(lo, hi, t0, t1, n10):
    m1 = hi + nn(hi.astype(BF), t1)
    m = lo - nn(m1.astype(BF), n10)
    return m + nn(m.astype(BF), t0), m1


def kernel(
    q, k, v, z, a, b, cq, ck, cv, alog, dtb, gain,
    out,
    rq, rk, rv, ra, rb, hq, hk, hv, zin, sz, xs, wq, wk, wv, walog, wdtb, wgain,
    masks, ccol, crow, brow, dec, nmat, tmat, ks, vs, kdt, mb, o0, gmat,
    dsend, asend, dmap, amap, pxd, pxa, pep, sfx, sfe, gds, gas, gdm, gam, state, ssend, sbuf, nb, fo,
    k_s, k_r, v_s, v_r, q_s, q_r, ab_s, ab_r, halo_s, halo_r, loc, zsem,
    d_s, d_r, a_s, a_r, yd_s, yd_r, ya_s, ya_r, st_s, st_r, ret_s, ret_r,
):
    ctx = lax.axis_index("ctx")
    me = lax.axis_index("head")
    nctx = lax.axis_size("ctx")
    yrow = ctx // GRP
    base = yrow * GRP
    mine = ctx - base
    nrow = nctx // GRP
    prev = lax.rem(ctx + nctx - 1, nctx)
    nxt = lax.rem(ctx + 1, nctx)

    def peer(d):
        return lax.rem(me + d, NH)

    def source(d):
        return lax.rem(me + NH - d, NH)

    KINDS = ((k, rk, hk, 512, D, k_s, k_r), (v, rv, hv, 1024, 2 * D, v_s, v_r), (q, rq, hq, 512, D, q_s, q_r))
    my_rows = pl.ds(aligned(me * BLK, BLK), BLK)

    def own_copies():
        cps = []
        for i, (src, dst) in enumerate(
            ((ck, wk), (cv, wv), (cq, wq), (alog, walog), (dtb, wdtb), (gain, wgain), (a, ra.at[me]), (b, rb.at[me]))
        ):
            cps.append(pltpu.make_async_copy(src, dst, loc.at[i]))
        for i, (src, dst, _, w, _, _, _) in enumerate(KINDS):
            cps.append(pltpu.make_async_copy(src.at[:, pl.ds(aligned(me * w, w), w)], dst.at[my_rows, :], loc.at[8 + i]))
        return cps

    for cp in own_copies():
        cp.start()
    zcopy = pltpu.make_async_copy(z, zin, zsem)
    zcopy.start()

    barrier = pltpu.get_barrier_semaphore()
    for d in range(1, NH):
        pl.semaphore_signal(barrier, inc=1, device_id={"head": peer(d)}, device_id_type=MESH)
    for d in range(1, GRP):
        pl.semaphore_signal(barrier, inc=1, device_id={"ctx": base + lax.rem(mine + d, GRP)}, device_id_type=MESH)
    for d in range(1, 4):
        pl.semaphore_signal(barrier, inc=1, device_id={"ctx": lax.rem(ctx + d * GRP, nctx)}, device_id_type=MESH)

    @pl.when(me < NH - 1)
    def _():
        pl.semaphore_signal(barrier, inc=1, device_id={"ctx": prev, "head": NH - 1}, device_id_type=MESH)

    @pl.when(me == NH - 1)
    def _():
        pl.semaphore_signal(barrier, inc=1, device_id={"ctx": prev}, device_id_type=MESH)
        for p in range(NH - 1):
            pl.semaphore_signal(barrier, inc=1, device_id={"ctx": nxt, "head": p}, device_id_type=MESH)
        pl.semaphore_signal(barrier, inc=1, device_id={"ctx": nxt}, device_id_type=MESH)

    r1 = lax.broadcasted_iota(jnp.int32, (D, D), 0)
    c1 = lax.broadcasted_iota(jnp.int32, (D, D), 1)
    gap = r1 ^ c1
    masks[0] = (r1 == c1).astype(F32).astype(BF)
    for i in range(7):
        masks[i + 1] = jnp.where((gap >= 2**i) & (gap < 2 ** (i + 1)) & (r1 > c1), -1.0, 0.0).astype(BF)
    pl.semaphore_wait(barrier, jnp.where(me == NH - 1, 3 + 7 + 3 + 1 + 4, 3 + 7 + 3 + 1))

    def ab_copy(d, i):
        src, dst = ((a, ra), (b, rb))[i]
        return remote(src, dst.at[me], ab_s.at[d - 1, i], ab_r.at[d - 1, i], {"head": peer(d)})

    def rows_copy(i, d, kh):
        src, dst, _, w, cw, ssem, rsem = KINDS[i]
        return remote(
            src.at[:, pl.ds(aligned(peer(d) * w + kh * cw, cw), cw)],
            dst.at[my_rows, pl.ds(aligned(kh * cw, cw), cw)],
            ssem.at[kh, d - 1], rsem.at[kh, d - 1], {"head": peer(d)},
        )

    def halo_copy(i, p):
        src, _, dst, w, _, _, _ = KINDS[i]
        where = {"ctx": nxt} if p == NH - 1 else {"ctx": nxt, "head": p}
        return remote(src.at[pl.ds(BLK - RIM, RIM), pl.ds(p * w, w)], dst, halo_s.at[p, i], halo_r.at[i], where)

    for d in (2, 1, 3):
        for i in range(2):
            ab_copy(d, i).start()
    for i in range(3):
        @pl.when(me == NH - 1)
        def _():
            for p in range(NH):
                halo_copy(i, p).start()

        @pl.loop(0, HK)
        def _(kh):
            for d in (2, 1, 3):
                rows_copy(i, d, kh).start()

    zcopy.wait()

    @pl.loop(0, 8)
    def _(i):
        cols = pl.ds(aligned(i * 512, 512), 512)
        zf = zin[:, cols].astype(F32)
        sz[:, cols] = zf * sigmoid(zf)

    for cp in own_copies():
        cp.wait()
    for d in range(1, NH):
        for i in range(2):
            ab_copy(d, i).wait_recv()
    sel = (
        lax.broadcasted_iota(jnp.int32, (HV, 32), 1) == lax.broadcasted_iota(jnp.int32, (HV, 32), 0) + me * HV
    ).astype(F32).astype(BF)
    eye8 = lax.broadcasted_iota(jnp.int32, (HV, HV), 0) == lax.broadcasted_iota(jnp.int32, (HV, HV), 1)

    def column(row):
        return jnp.sum(jnp.where(eye8, jnp.broadcast_to(row, (HV, HV)), 0.0), axis=1, keepdims=True)

    a_row = jnp.concatenate([nn(sel, ra[s]) for s in range(NH)], axis=1) + column(wdtb[...])
    b_row = jnp.concatenate([nn(sel, rb[s]) for s in range(NH)], axis=1)
    g_row = -column(jnp.exp(walog[...])) * (jnp.maximum(a_row, 0.0) + jnp.log1p(jnp.exp(-jnp.abs(a_row))))
    beta_row = sigmoid(b_row)
    row = lax.broadcasted_iota(jnp.int32, (C, C), 0)
    col = lax.broadcasted_iota(jnp.int32, (C, C), 1)
    c_row = nn(g_row, (row <= col).astype(F32), HIGHEST)
    both = jnp.transpose(jnp.concatenate([c_row, beta_row], axis=0))
    for kh in range(HK):
        ccol[kh, :, 0:2] = both[:, 2 * kh : 2 * kh + 2]
        ccol[kh, :, 2:4] = both[:, HV + 2 * kh : HV + 2 * kh + 2]
    for h in range(HV):
        crow[h] = c_row[h : h + 1, :]
        brow[h] = beta_row[h : h + 1, :]
    inside = jnp.where(ctx > 0, 1.0, 0.0).astype(F32)

    def conv_silu(i, taps, kh):
        _, rows, halo, _, cw, _, _ = KINDS[i]
        cols = pl.ds(aligned(kh * cw, cw), cw)
        here = pl.ds(0, cw)
        for d in range(1, NH):
            rows_copy(i, d, kh).wait_recv()
        xs[pl.ds(0, RIM), here] = halo[:, cols].astype(F32) * inside
        xs[pl.ds(RIM, C), here] = rows[:, cols].astype(F32)
        w = taps[:, cols]
        total = w[0:1, :] * xs[pl.ds(RIM - 3, C), here]
        for j in range(1, 4):
            total = total + w[j : j + 1, :] * xs[pl.ds(RIM - 3 + j, C), here]
        return total * sigmoid(total)

    def unit(x, factor):
        return (x * (lax.rsqrt(jnp.sum(x * x, axis=-1, keepdims=True) + 1e-6) * factor)).astype(BF)

    halo_copy(0, 0).wait_recv()

    @pl.loop(0, HK)
    def _(kh):
        kn = unit(conv_silu(0, wk, kh), 1.0)
        ks[kh] = kn
        kt = jnp.transpose(kn.astype(F32))
        kk00, kk1 = nt(kn[:D], kn[:D]), nt(kn[D:], kn)
        cc = ccol[kh]
        low = lax.broadcasted_iota(jnp.int32, (D, D), 0) >= lax.broadcasted_iota(jnp.int32, (D, D), 1)
        for j in range(2):
            h = 2 * kh + j
            cj, bj, cr = cc[:, j : j + 1], cc[:, 2 + j : 3 + j], crow[h]
            d00 = jnp.exp(jnp.where(low, cj[:D] - cr[:, :D], NEG))
            d10 = jnp.exp(cj[D:] - cr[:, :D])
            d11 = jnp.exp(jnp.where(low, cj[D:] - cr[:, D:], NEG))
            dec[h, 0], dec[h, 1], dec[h, 2] = d00, d10, d11
            nmat[h, 0] = (bj[:D] * d00 * kk00).astype(BF)
            nmat[h, 1] = (bj[D:] * d10 * kk1[:, :D]).astype(BF)
            nmat[h, 2] = (bj[D:] * d11 * kk1[:, D:]).astype(BF)
            kdt[h] = (kt * jnp.exp(cr[:, C - 1 : C] - cr)).astype(BF)

    chains = [(h, i) for h in range(HV) for i in (0, 2)]
    ts = [masks[0] + nmat[h, i] * masks[1] for h, i in chains]
    for level in range(2, 8):
        left = [nn(t, nmat[h, i] * masks[level]).astype(BF) for t, (h, i) in zip(ts, chains)]
        ts = [t + nn(x, t).astype(BF) for t, x in zip(ts, left)]
    for t, (h, i) in zip(ts, chains):
        tmat[h, i // 2] = t - masks[0]

    def d_copy(m, slot):
        return remote(dsend.at[m], dmap.at[mine], d_s.at[m], d_r.at[slot], {"ctx": base + m})

    def a_copy(m, slot):
        return remote(asend.at[m], amap.at[mine], a_s.at[m], a_r.at[slot], {"ctx": base + m})

    @pl.loop(0, HK)
    def _(kh):
        for j in range(2):
            h = 2 * kh + j
            x = kdt[h].astype(F32)
            m0, m1 = times_inverse(x[:, :D], x[:, D:], tmat[h, 0], tmat[h, 1], nmat[h, 1])
            cr = crow[h]
            m = jnp.concatenate([m0, m1], axis=1) * brow[h]
            mb[h] = m.astype(BF)
            dsend[h, pl.ds(0, D), :] = (-nn((m * jnp.exp(cr)).astype(BF), ks[kh])).astype(BF)
            store_exact(dsend.at[h], jnp.broadcast_to(jnp.exp(cr[:, C - 1 : C]), (1, D)))
        for j in range(2):
            h = 2 * kh + j

            @pl.when(h != mine)
            def _():
                d_copy(h, mine).start()

            @pl.when(h == mine)
            def _():
                dmap[mine] = dsend[h]

    halo_copy(1, 0).wait_recv()

    @pl.loop(0, HK)
    def _(kh):
        vn = conv_silu(1, wv, kh).astype(BF)
        vs[kh] = vn
        for j in range(2):
            h = 2 * kh + j
            asend[h] = nn(mb[h], vn[:, j * D : (j + 1) * D]).astype(BF)
        for j in range(2):
            h = 2 * kh + j

            @pl.when(h != mine)
            def _():
                a_copy(h, mine).start()

            @pl.when(h == mine)
            def _():
                amap[mine] = asend[h]

    def wait_from(copy, i):
        @pl.when(mine != i)
        def _():
            copy(i, i).wait_recv()

    for i in range(GRP):
        wait_from(d_copy, i)
    lin = [dmap[i, pl.ds(0, D), :] for i in range(GRP)]
    decays = [load_exact(dmap.at[i]) for i in range(GRP)]
    xd, ep = lin[0].astype(F32), decays[0]
    sd, es = lin[GRP - 1].astype(F32), decays[GRP - 1]
    pxd[0] = jnp.zeros((D, D), BF)
    pep[0] = jnp.ones((1, D), F32)
    for i in range(1, GRP):
        xb = xd.astype(BF)
        pxd[i] = xb
        pep[i] = ep
        xd = decays[i] * xd + nn(lin[i], xb) + ep * lin[i].astype(F32)
        ep = ep * decays[i]
        m = GRP - 1 - i
        sb = sd.astype(BF)
        sfx[:, m * D : (m + 1) * D] = sb
        sfe[m] = es
        if m > 0:
            sd = decays[m] * sd + nn(sb, lin[m]) + es * lin[m].astype(F32)
            es = es * decays[m]
    gds[pl.ds(0, D), :] = xd.astype(BF)
    store_exact(gds, ep)

    def yd_copy(d):
        return remote(gds, gdm.at[yrow], yd_s.at[d - 1], yd_r.at[yrow], {"ctx": lax.rem(ctx + d * GRP, nctx)})

    def ya_copy(d):
        return remote(gas, gam.at[yrow], ya_s.at[d - 1], ya_r.at[yrow], {"ctx": lax.rem(ctx + d * GRP, nctx)})

    for d in range(1, 4):
        @pl.when((yrow > 0) & (yrow + d < nrow))
        def _():
            yd_copy(d).start()

    halo_copy(2, 0).wait_recv()

    def own_tokens(kh):
        qn = unit(conv_silu(2, wq, kh), D ** -0.5)
        kn, vn = ks[kh], vs[kh]
        qk00, qk1 = nt(qn[:D], kn[:D]), nt(qn[D:], kn)
        qf = qn.astype(F32)
        for j in range(2):
            h = 2 * kh + j
            grow = jnp.exp(ccol[kh][:, j : j + 1])
            bt = brow[h]
            btg = bt * jnp.exp(crow[h])
            vj = vn[:, j * D : (j + 1) * D]
            p00 = dec[h, 0] * qk00
            p00 = p00 + nn(p00.astype(BF), tmat[h, 0])
            p10, p11 = times_inverse(
                dec[h, 1] * qk1[:, :D], dec[h, 2] * qk1[:, D:], tmat[h, 0], tmat[h, 1], nmat[h, 1]
            )
            p1 = jnp.concatenate([p10, p11], axis=1)
            o0[h, pl.ds(0, D), :] = nn((p00 * bt[:, :D]).astype(BF), vj[:D])
            o0[h, pl.ds(D, D), :] = nn((p1 * bt).astype(BF), vj)
            gmat[h, pl.ds(0, D), :] = (grow[:D] * qf[:D] - nn((p00 * btg[:, :D]).astype(BF), kn[:D])).astype(BF)
            gmat[h, pl.ds(D, D), :] = (grow[D:] * qf[D:] - nn((p1 * btg).astype(BF), kn)).astype(BF)

    pl.loop(0, 2)(own_tokens)

    for i in range(GRP):
        wait_from(a_copy, i)
    add = [amap[i] for i in range(GRP)]
    total = add[GRP - 1].astype(F32) + nn(sfx[...], jnp.concatenate(add[: GRP - 1], axis=0))
    for i in range(GRP - 1):
        total = total + sfe[i] * add[i].astype(F32)
    gas[...] = total.astype(BF)
    for d in range(1, 4):
        @pl.when(yrow + d < nrow)
        def _():
            ya_copy(d).start()

    xa = add[0].astype(F32)
    pxa[0] = jnp.zeros((D, D), F32)
    for i in range(1, GRP):
        pxa[i] = xa
        if i < GRP - 1:
            xa = decays[i] * xa + nn(lin[i], xa.astype(BF)) + add[i].astype(F32)
    pl.loop(2, HK)(own_tokens)

    state[...] = jnp.zeros_like(state)
    for yy in range(3):
        @pl.when(yy < yrow)
        def _():
            remote(gas, gam.at[yy], ya_s.at[0], ya_r.at[yy], {"ctx": prev}).wait_recv()
            if yy == 0:
                state[...] = gam[0].astype(F32)
            else:
                remote(gds, gdm.at[yy], yd_s.at[0], yd_r.at[yy], {"ctx": prev}).wait_recv()
                s_now = state[...]
                state[...] = (
                    load_exact(gdm.at[yy]) * s_now
                    + nn(gdm[yy, pl.ds(0, D), :], s_now.astype(BF))
                    + gam[yy].astype(F32)
                )

    def state_copy(i, slot):
        return remote(ssend.at[i], sbuf.at[mine], st_s.at[i], st_r.at[slot], {"ctx": base + i})

    s_in = state[...]
    sb = s_in.astype(BF)
    for t in range(1, GRP + 1):
        i = lax.rem(mine + t, GRP)
        s_i = (pep[i] * s_in + nn(pxd[i], sb) + pxa[i]).astype(BF)
        if t < GRP:
            ssend[i] = s_i
            state_copy(i, mine).start()
        else:
            sbuf[mine] = s_i

    def ret_copy(d, h, slot):
        return remote(
            nb.at[pl.ds(aligned(peer(d) * BLK, BLK), BLK), pl.ds(aligned(h * D, D), D)],
            fo.at[:, pl.ds(aligned(me * HV * D + h * D, D), D)],
            ret_s.at[h, d - 1], ret_r.at[h, slot], {"head": peer(d)},
        )

    @pl.loop(0, GRP)
    def _(t):
        h = lax.rem(mine + GRP - t, GRP)

        @pl.when(t > 0)
        def _():
            state_copy(h, h).wait_recv()

        core = o0[h] + nn(gmat[h], sbuf[h])
        inv = lax.rsqrt(jnp.mean(core * core, axis=-1, keepdims=True) + 1e-6)
        nb[:, pl.ds(aligned(h * D, D), D)] = (core * inv * wgain[...]).astype(BF)
        for d in (2, 1, 3):
            ret_copy(d, h, d - 1).start()

    def gate(src, rows_of):
        @pl.loop(0, 2)
        def _(i):
            cols = pl.ds(aligned(src * HV * D + i * 512, 512), 512)
            out[:, cols] = (rows_of(cols, i) * sz[:, cols]).astype(BF)

    gate(me, lambda cols, i: nb[my_rows, pl.ds(aligned(i * 512, 512), 512)].astype(F32))
    for d in (1, 3, 2):
        @pl.loop(0, HV)
        def _(h):
            ret_copy(d, h, d - 1).wait_recv()

        gate(source(d), lambda cols, i: fo[:, cols].astype(F32))

    for d in range(1, NH):
        for i in range(2):
            ab_copy(d, i).wait_send()

        @pl.loop(0, HK)
        def _(kh):
            for i in range(3):
                rows_copy(i, d, kh).wait_send()

        @pl.loop(0, HV)
        def _(h):
            ret_copy(d, h, d - 1).wait_send()

        @pl.when(yrow + d < nrow)
        def _():
            ya_copy(d).wait_send()

        @pl.when((yrow > 0) & (yrow + d < nrow))
        def _():
            yd_copy(d).wait_send()

    @pl.when(me == NH - 1)
    def _():
        for p in range(NH):
            for i in range(3):
                halo_copy(i, p).wait_send()

    @pl.loop(0, GRP)
    def _(i):
        @pl.when(i != mine)
        def _():
            d_copy(i, mine).wait_send()
            a_copy(i, mine).wait_send()
            state_copy(i, mine).wait_send()


def local(q, k, v, z, a, b, cq, ck, cv, alog, dtb, gain):
    any_spec = pl.BlockSpec(memory_space=pl.ANY)
    dma = pltpu.SemaphoreType.DMA

    def bf(*shape):
        return pltpu.VMEM(shape, BF)

    def f32(*shape):
        return pltpu.VMEM(shape, F32)

    scratch = dict(
        rq=bf(C, 512), rk=bf(C, 512), rv=bf(C, 1024), ra=bf(NH, 32, BLK), rb=bf(NH, 32, BLK),
        hq=bf(RIM, 512), hk=bf(RIM, 512), hv=bf(RIM, 1024), zin=bf(BLK, 4096), sz=f32(BLK, 4096), xs=f32(C + RIM, 256),
        wq=f32(4, 512), wk=f32(4, 512), wv=f32(4, 1024), walog=f32(1, HV), wdtb=f32(1, HV), wgain=f32(1, D),
        masks=bf(8, D, D), ccol=f32(HK, C, 4), crow=f32(HV, 1, C), brow=f32(HV, 1, C),
        dec=f32(HV, 3, D, D), nmat=bf(HV, 3, D, D), tmat=bf(HV, 2, D, D), ks=bf(HK, C, D), vs=bf(HK, C, 2 * D),
        kdt=bf(HV, D, C), mb=bf(HV, D, C), o0=f32(HV, C, D), gmat=bf(HV, C, D),
        dsend=bf(HV, D + 16, D), asend=bf(HV, D, D), dmap=bf(GRP, D + 16, D), amap=bf(GRP, D, D),
        pxd=bf(GRP, D, D), pxa=f32(GRP, D, D), pep=f32(GRP, 1, D), sfx=bf(D, (GRP - 1) * D), sfe=f32(GRP, 1, D),
        gds=bf(D + 16, D), gas=bf(D, D), gdm=bf(4, D + 16, D), gam=bf(4, D, D),
        state=f32(D, D), ssend=bf(GRP, D, D), sbuf=bf(HV, D, D), nb=bf(C, HV * D), fo=bf(BLK, 4 * HV * D),
        k_s=dma((HK, 3)), k_r=dma((HK, 3)), v_s=dma((HK, 3)), v_r=dma((HK, 3)), q_s=dma((HK, 3)), q_r=dma((HK, 3)),
        ab_s=dma((3, 2)), ab_r=dma((3, 2)), halo_s=dma((4, 3)), halo_r=dma((3,)), loc=dma((11,)), zsem=dma,
        d_s=dma((GRP,)), d_r=dma((GRP,)), a_s=dma((GRP,)), a_r=dma((GRP,)),
        yd_s=dma((3,)), yd_r=dma((4,)), ya_s=dma((3,)), ya_r=dma((4,)),
        st_s=dma((GRP,)), st_r=dma((GRP,)), ret_s=dma((HV, 3)), ret_r=dma((HV, 3)),
    )
    return pl.pallas_call(
        kernel,
        out_shape=jax.ShapeDtypeStruct((BLK, 4 * HV * D), BF),
        in_specs=[any_spec] * 12,
        out_specs=pl.BlockSpec(memory_space=pltpu.VMEM),
        scratch_shapes=list(scratch.values()),
        compiler_params=pltpu.CompilerParams(
            collective_id=0, has_side_effects=True, vmem_limit_bytes=67043328
        ),
    )(q, k, v, z, a.T, b.T, cq, ck, cv, alog.reshape(1, HV), dtb.reshape(1, HV), gain.reshape(1, D))


def solution(mesh):
    rows = P(("ctx", "head"), None)
    placed = (rows,) * 6 + (P(None, "head"),) * 3 + (P("head"), P("head"), P())
    return jax.shard_map(local, mesh=mesh, in_specs=placed, out_specs=rows, check_vma=False)
```

```python
import functools

import jax
import jax.numpy as jnp
from jax import lax
from jax.experimental import pallas as pl
from jax.experimental.pallas import tpu as pltpu
from jax.sharding import PartitionSpec as P

MESH = pl.DeviceIdType.MESH
F32 = jnp.float32
BF = jnp.bfloat16
HIGHEST = lax.Precision.HIGHEST

D = 128
BLK = 64
C = 256
HK = 4
HV = 8
NH = 4
GRP = 8
RIM = 8
NEG = -1e30


def nn(a, b, precision=None):
    return lax.dot_general(
        a, b, (((1,), (0,)), ((), ())), precision=precision, preferred_element_type=F32
    )


def nt(a, b):
    return lax.dot_general(a, b, (((1,), (1,)), ((), ())), preferred_element_type=F32)


def sigmoid(x):
    return 1.0 / (1.0 + jnp.exp(-x))


def remote(src, dst, send, recv, where):
    return pltpu.make_async_remote_copy(
        src_ref=src, dst_ref=dst, send_sem=send, recv_sem=recv, device_id=where, device_id_type=MESH
    )


def aligned(x, n):
    return pl.multiple_of(x, n)


def store_exact(ref, row):
    wide = jnp.broadcast_to(row, (16, D))
    e1 = wide.astype(BF).astype(F32)
    e2 = (wide - e1).astype(BF).astype(F32)
    e3 = wide - e1 - e2
    i = lax.broadcasted_iota(jnp.int32, (16, D), 0)
    ref[pl.ds(D, 16), :] = jnp.where(i == 0, e1, jnp.where(i == 1, e2, jnp.where(i == 2, e3, 0.0))).astype(BF)


def load_exact(ref):
    p = ref[pl.ds(D, 16), :].astype(F32)
    return p[0:1, :] + p[1:2, :] + p[2:3, :]


def times_inverse(lo, hi, t0, t1, n10):
    m1 = hi + nn(hi.astype(BF), t1)
    m = lo - nn(m1.astype(BF), n10)
    return m + nn(m.astype(BF), t0), m1


def kernel(
    q, k, v, a, b, cq, ck, cv, alog, dtb, gain,
    out,
    rq, rk, rv, ra, rb, hq, hk, hv, tq, tk, tv, xs, wq, wk, wv, walog, wdtb, wgain,
    masks, ccol, crow, brow, dec, nmat, tmat, ks, vs, kdt, mb, o0, gmat,
    dsend, asend, dmap, amap, pxd, pxa, pep, sfx, sfe, gds, gas, gdm, gam, state, ssend, sbuf, nb,
    k_s, k_r, v_s, v_r, q_s, q_r, ab_s, ab_r, tail_s, tail_r, halo_s, halo_r, loc,
    d_s, d_r, a_s, a_r, yd_s, yd_r, ya_s, ya_r, st_s, st_r, ret_s, ret_r,
):
    ctx = lax.axis_index("ctx")
    me = lax.axis_index("head")
    nctx = lax.axis_size("ctx")
    yrow = ctx // GRP
    base = yrow * GRP
    mine = ctx - base
    nrow = nctx // GRP
    prev = lax.rem(ctx + nctx - 1, nctx)
    nxt = lax.rem(ctx + 1, nctx)

    def owner(h):
        return lax.rem(h, 4) * 2 + h // 4

    def head_of(m):
        return lax.rem(m, 2) * 4 + m // 2

    my_head = head_of(mine)

    def peer(d):
        return lax.rem(me + d, NH)

    def source(d):
        return lax.rem(me + NH - d, NH)

    KINDS = (
        (k, rk, hk, tk, 512, D, k_s, k_r),
        (v, rv, hv, tv, 1024, 2 * D, v_s, v_r),
        (q, rq, hq, tq, 512, D, q_s, q_r),
    )
    my_rows = pl.ds(aligned(me * BLK, BLK), BLK)

    def own_copies():
        cps = []
        for i, (src, dst) in enumerate(
            ((ck, wk), (cv, wv), (cq, wq), (alog, walog), (dtb, wdtb), (gain, wgain), (a, ra.at[me]), (b, rb.at[me]))
        ):
            cps.append(pltpu.make_async_copy(src, dst, loc.at[i]))
        for i, (src, dst, _, _, w, _, _, _) in enumerate(KINDS):
            cps.append(pltpu.make_async_copy(src.at[:, pl.ds(aligned(me * w, w), w)], dst.at[my_rows, :], loc.at[8 + i]))
        return cps

    for cp in own_copies():
        cp.start()

    barrier = pltpu.get_barrier_semaphore()
    for d in range(1, NH):
        pl.semaphore_signal(barrier, inc=1, device_id={"head": peer(d)}, device_id_type=MESH)
    for d in range(1, GRP):
        pl.semaphore_signal(barrier, inc=1, device_id={"ctx": base + lax.rem(mine + d, GRP)}, device_id_type=MESH)
    for d in range(1, 4):
        pl.semaphore_signal(barrier, inc=1, device_id={"ctx": lax.rem(ctx + d * GRP, nctx)}, device_id_type=MESH)

    for near in (prev, nxt):
        pl.semaphore_signal(barrier, inc=1, device_id={"ctx": near}, device_id_type=MESH)
    r1 = lax.broadcasted_iota(jnp.int32, (D, D), 0)
    c1 = lax.broadcasted_iota(jnp.int32, (D, D), 1)
    gap = r1 ^ c1
    masks[0] = (r1 == c1).astype(F32).astype(BF)
    for i in range(7):
        masks[i + 1] = jnp.where((gap >= 2**i) & (gap < 2 ** (i + 1)) & (r1 > c1), -1.0, 0.0).astype(BF)
    pl.semaphore_wait(barrier, 3 + 7 + 3 + 2)

    def ab_copy(d, i):
        src, dst = ((a, ra), (b, rb))[i]
        return remote(src, dst.at[me], ab_s.at[d - 1, i], ab_r.at[d - 1, i], {"head": peer(d)})

    def rows_copy(i, d, kh):
        src, dst, _, _, w, cw, ssem, rsem = KINDS[i]
        return remote(
            src.at[:, pl.ds(aligned(peer(d) * w + kh * cw, cw), cw)],
            dst.at[my_rows, pl.ds(aligned(kh * cw, cw), cw)],
            ssem.at[kh, d - 1], rsem.at[kh, d - 1], {"head": peer(d)},
        )

    def tail_copy(i, d):
        src, _, _, dst, w, _, _, _ = KINDS[i]
        return remote(
            src.at[pl.ds(BLK - RIM, RIM), pl.ds(aligned(peer(d) * w, w), w)], dst, tail_s.at[i, d - 1], tail_r.at[i],
            {"head": peer(d)},
        )

    def halo_copy(i):
        _, _, dst, src, _, _, _, _ = KINDS[i]
        return remote(src, dst, halo_s.at[i], halo_r.at[i], {"ctx": nxt})

    def halo_first(i):
        src, _, dst, _, w, _, _, _ = KINDS[i]
        return remote(
            src.at[pl.ds(BLK - RIM, RIM), pl.ds((NH - 1) * w, w)], dst, halo_s.at[i], halo_r.at[i], {"ctx": nxt}
        )

    def send_tails(*kinds):
        @pl.when(me == NH - 1)
        def _():
            for i in kinds:
                for d in (2, 1, 3):
                    tail_copy(i, d).start()
            for i in kinds:
                halo_first(i).start()

    def pass_tails(*kinds):
        @pl.when(me < NH - 1)
        def _():
            for i in kinds:
                tail_copy(i, 1).wait_recv()
                halo_copy(i).start()

    for d in (2, 1, 3):
        for i in range(2):
            ab_copy(d, i).start()
    send_tails(0, 1, 2)
    for i in range(3):
        @pl.loop(0, HK)
        def _(kh):
            for d in (2, 1, 3):
                rows_copy(i, d, kh).start()

        if i == 0:
            pass_tails(0, 1, 2)

    for cp in own_copies():
        cp.wait()
    for d in range(1, NH):
        for i in range(2):
            ab_copy(d, i).wait_recv()
    sel = (
        lax.broadcasted_iota(jnp.int32, (HV, 32), 1) == lax.broadcasted_iota(jnp.int32, (HV, 32), 0) + me * HV
    ).astype(F32).astype(BF)
    eye8 = lax.broadcasted_iota(jnp.int32, (HV, HV), 0) == lax.broadcasted_iota(jnp.int32, (HV, HV), 1)

    def column(row):
        return jnp.sum(jnp.where(eye8, jnp.broadcast_to(row, (HV, HV)), 0.0), axis=1, keepdims=True)

    a_row = jnp.concatenate([nn(sel, ra[s]) for s in range(NH)], axis=1) + column(wdtb[...])
    b_row = jnp.concatenate([nn(sel, rb[s]) for s in range(NH)], axis=1)
    g_row = -column(jnp.exp(walog[...])) * (jnp.maximum(a_row, 0.0) + jnp.log1p(jnp.exp(-jnp.abs(a_row))))
    beta_row = sigmoid(b_row)
    row = lax.broadcasted_iota(jnp.int32, (C, C), 0)
    col = lax.broadcasted_iota(jnp.int32, (C, C), 1)
    c_row = nn(g_row, (row <= col).astype(F32), HIGHEST)
    both = jnp.transpose(jnp.concatenate([c_row, beta_row], axis=0))
    for kh in range(HK):
        ccol[kh, :, 0:2] = both[:, 2 * kh : 2 * kh + 2]
        ccol[kh, :, 2:4] = both[:, HV + 2 * kh : HV + 2 * kh + 2]
    for h in range(HV):
        crow[h] = c_row[h : h + 1, :]
        brow[h] = beta_row[h : h + 1, :]
    inside = jnp.where(ctx > 0, 1.0, 0.0).astype(F32)

    def arrived(i, kh):
        for d in range(1, NH):
            rows_copy(i, d, kh).wait_recv()

    def conv_silu(i, taps, kh):
        _, rows, halo, _, _, cw, _, _ = KINDS[i]
        cols = pl.ds(aligned(kh * cw, cw), cw)
        here = pl.ds(0, cw)
        xs[pl.ds(0, RIM), here] = halo[:, cols].astype(F32) * inside
        xs[pl.ds(RIM, C), here] = rows[:, cols].astype(F32)
        w = taps[:, cols]
        total = w[0:1, :] * xs[pl.ds(RIM - 3, C), here]
        for j in range(1, 4):
            total = total + w[j : j + 1, :] * xs[pl.ds(RIM - 3 + j, C), here]
        return total * sigmoid(total)

    def unit(x, factor):
        return (x * (lax.rsqrt(jnp.sum(x * x, axis=-1, keepdims=True) + 1e-6) * factor)).astype(BF)

    halo_copy(0).wait_recv()

    def key_head(kh):
        arrived(0, kh)
        kn = unit(conv_silu(0, wk, kh), 1.0)
        ks[kh] = kn
        kt = jnp.transpose(kn.astype(F32))
        kk00, kk1 = nt(kn[:D], kn[:D]), nt(kn[D:], kn)
        cc = ccol[kh]
        low = lax.broadcasted_iota(jnp.int32, (D, D), 0) >= lax.broadcasted_iota(jnp.int32, (D, D), 1)
        for j in range(2):
            h = 2 * kh + j
            cj, bj, cr = cc[:, j : j + 1], cc[:, 2 + j : 3 + j], crow[h]
            d00 = jnp.exp(jnp.where(low, cj[:D] - cr[:, :D], NEG))
            d10 = jnp.exp(cj[D:] - cr[:, :D])
            d11 = jnp.exp(jnp.where(low, cj[D:] - cr[:, D:], NEG))
            dec[h, 0], dec[h, 1], dec[h, 2] = d00, d10, d11
            nmat[h, 0] = (bj[:D] * d00 * kk00).astype(BF)
            nmat[h, 1] = (bj[D:] * d10 * kk1[:, :D]).astype(BF)
            nmat[h, 2] = (bj[D:] * d11 * kk1[:, D:]).astype(BF)
            kdt[h] = (kt * jnp.exp(cr[:, C - 1 : C] - cr)).astype(BF)

    def d_copy(h, slot):
        return remote(dsend.at[h], dmap.at[mine], d_s.at[h], d_r.at[slot], {"ctx": base + owner(h)})

    def a_copy(h, slot):
        return remote(asend.at[h], amap.at[mine], a_s.at[h], a_r.at[slot], {"ctx": base + owner(h)})

    def hand_over(copy, kept, sent, h):
        @pl.when(h != my_head)
        def _():
            copy(h, mine).start()

        @pl.when(h == my_head)
        def _():
            kept[mine] = sent[h]

    @pl.loop(0, 2)
    def _(half):
        pl.loop(2 * half, 2 * half + 2)(key_head)

        heads = [4 * half + x for x in range(4)]
        chains = [(h, i) for h in heads for i in (0, 2)]
        ts = [masks[0] + nmat[h, i] * masks[1] for h, i in chains]
        for level in range(2, 8):
            left = [nn(t, nmat[h, i] * masks[level]).astype(BF) for t, (h, i) in zip(ts, chains)]
            ts = [t + nn(x, t).astype(BF) for t, x in zip(ts, left)]
        for t, (h, i) in zip(ts, chains):
            tmat[h, i // 2] = t - masks[0]

        m1 = [kdt[h, :, D:].astype(F32) + nn(kdt[h, :, D:], tmat[h, 1]) for h in heads]
        m0 = [kdt[h, :, :D].astype(F32) - nn(x.astype(BF), nmat[h, 1]) for x, h in zip(m1, heads)]
        m0 = [x + nn(x.astype(BF), tmat[h, 0]) for x, h in zip(m0, heads)]
        for x, h in enumerate(heads):
            cr = crow[h]
            m = jnp.concatenate([m0[x], m1[x]], axis=1) * brow[h]
            mb[h] = m.astype(BF)
            dsend[h, pl.ds(0, D), :] = (-nn((m * jnp.exp(cr)).astype(BF), ks[2 * half + x // 2])).astype(BF)
            store_exact(dsend.at[h], jnp.broadcast_to(jnp.exp(cr[:, C - 1 : C]), (1, D)))
        for h in heads:
            hand_over(d_copy, dmap, dsend, h)

    halo_copy(1).wait_recv()

    @pl.loop(0, HK)
    def _(kh):
        arrived(1, kh)
        vn = conv_silu(1, wv, kh).astype(BF)
        vs[kh] = vn
        for j in range(2):
            h = 2 * kh + j
            asend[h] = nn(mb[h], vn[:, j * D : (j + 1) * D]).astype(BF)
        for j in range(2):
            hand_over(a_copy, amap, asend, 2 * kh + j)

    halo_copy(2).wait_recv()

    def own_tokens(pair):
        for kh in (2 * pair, 2 * pair + 1):
            arrived(2, kh)
        qn = [unit(conv_silu(2, wq, kh), D ** -0.5) for kh in (2 * pair, 2 * pair + 1)]
        todo = []
        for g in range(2):
            kh = 2 * pair + g
            kn = ks[kh]
            qk00, qk1 = nt(qn[g][:D], kn[:D]), nt(qn[g][D:], kn)
            for j in range(2):
                h = 2 * kh + j
                todo.append((kh, j, h, g, dec[h, 0] * qk00, dec[h, 1] * qk1[:, :D], dec[h, 2] * qk1[:, D:]))
        m1 = [hi + nn(hi.astype(BF), tmat[h, 1]) for _, _, h, _, _, _, hi in todo]
        m0 = [lo - nn(x.astype(BF), nmat[h, 1]) for x, (_, _, h, _, _, lo, _) in zip(m1, todo)]
        p00 = [top + nn(top.astype(BF), tmat[h, 0]) for _, _, h, _, top, _, _ in todo]
        m0 = [x + nn(x.astype(BF), tmat[h, 0]) for x, (_, _, h, _, _, _, _) in zip(m0, todo)]
        for n, (kh, j, h, g, _, _, _) in enumerate(todo):
            grow = jnp.exp(ccol[kh][:, j : j + 1])
            bt = brow[h]
            btg = bt * jnp.exp(crow[h])
            kn, vj, qf = ks[kh], vs[kh][:, j * D : (j + 1) * D], qn[g].astype(F32)
            p1 = jnp.concatenate([m0[n], m1[n]], axis=1)
            o0[h, pl.ds(0, D), :] = nn((p00[n] * bt[:, :D]).astype(BF), vj[:D])
            o0[h, pl.ds(D, D), :] = nn((p1 * bt).astype(BF), vj)
            gmat[h, pl.ds(0, D), :] = (grow[:D] * qf[:D] - nn((p00[n] * btg[:, :D]).astype(BF), kn[:D])).astype(BF)
            gmat[h, pl.ds(D, D), :] = (grow[D:] * qf[D:] - nn((p1 * btg).astype(BF), kn)).astype(BF)

    own_tokens(0)

    def wait_from(copy, i):
        @pl.when(mine != i)
        def _():
            copy(i, i).wait_recv()

    for i in range(GRP):
        wait_from(d_copy, i)
    lin = [dmap[i, pl.ds(0, D), :] for i in range(GRP)]
    decays = [load_exact(dmap.at[i]) for i in range(GRP)]
    xd, ep = lin[0].astype(F32), decays[0]
    sd, es = lin[GRP - 1].astype(F32), decays[GRP - 1]
    pxd[0] = jnp.zeros((D, D), BF)
    pep[0] = jnp.ones((1, D), F32)
    for i in range(1, GRP):
        xb = xd.astype(BF)
        pxd[i] = xb
        pep[i] = ep
        xd = decays[i] * xd + nn(lin[i], xb) + ep * lin[i].astype(F32)
        ep = ep * decays[i]
        m = GRP - 1 - i
        sb = sd.astype(BF)
        sfx[:, m * D : (m + 1) * D] = sb
        sfe[m] = es
        if m > 0:
            sd = decays[m] * sd + nn(sb, lin[m]) + es * lin[m].astype(F32)
            es = es * decays[m]
    gds[pl.ds(0, D), :] = xd.astype(BF)
    store_exact(gds, ep)

    def yd_copy(d):
        return remote(gds, gdm.at[yrow], yd_s.at[d - 1], yd_r.at[yrow], {"ctx": lax.rem(ctx + d * GRP, nctx)})

    def ya_copy(d):
        return remote(gas, gam.at[yrow], ya_s.at[d - 1], ya_r.at[yrow], {"ctx": lax.rem(ctx + d * GRP, nctx)})

    for d in range(1, 4):
        @pl.when((yrow > 0) & (yrow + d < nrow))
        def _():
            yd_copy(d).start()

    for i in range(GRP):
        wait_from(a_copy, i)
    add = [amap[i] for i in range(GRP)]
    total = add[GRP - 1].astype(F32) + nn(sfx[...], jnp.concatenate(add[: GRP - 1], axis=0))
    for i in range(GRP - 1):
        total = total + sfe[i] * add[i].astype(F32)
    gas[...] = total.astype(BF)
    for d in range(1, 4):
        @pl.when(yrow + d < nrow)
        def _():
            ya_copy(d).start()

    xa = add[0].astype(F32)
    pxa[0] = jnp.zeros((D, D), F32)
    for i in range(1, GRP):
        pxa[i] = xa
        if i < GRP - 1:
            xa = decays[i] * xa + nn(lin[i], xa.astype(BF)) + add[i].astype(F32)
    own_tokens(1)

    state[...] = jnp.zeros_like(state)
    for yy in range(3):
        @pl.when(yy < yrow)
        def _():
            remote(gas, gam.at[yy], ya_s.at[0], ya_r.at[yy], {"ctx": prev}).wait_recv()
            if yy == 0:
                state[...] = gam[0].astype(F32)
            else:
                remote(gds, gdm.at[yy], yd_s.at[0], yd_r.at[yy], {"ctx": prev}).wait_recv()
                s_now = state[...]
                state[...] = (
                    load_exact(gdm.at[yy]) * s_now
                    + nn(gdm[yy, pl.ds(0, D), :], s_now.astype(BF))
                    + gam[yy].astype(F32)
                )

    def state_copy(i, slot):
        return remote(ssend.at[i], sbuf.at[my_head], st_s.at[i], st_r.at[slot], {"ctx": base + i})

    s_in = state[...]
    moved = nn(jnp.concatenate([pxd[i] for i in range(GRP)], axis=0), s_in.astype(BF))
    for i in range(GRP):
        ssend[i] = (pep[i] * s_in + moved[i * D : (i + 1) * D] + pxa[i]).astype(BF)
    for t in range(1, GRP):
        state_copy(lax.rem(mine + t, GRP), my_head).start()
    sbuf[my_head] = ssend[mine]

    def ret_copy(d, h, slot):
        return remote(
            nb.at[pl.ds(aligned(peer(d) * BLK, BLK), BLK), pl.ds(aligned(h * D, D), D)],
            out.at[:, pl.ds(aligned(me * HV * D + h * D, D), D)],
            ret_s.at[h, d - 1], ret_r.at[h, slot], {"head": peer(d)},
        )

    @pl.loop(0, GRP)
    def _(t):
        h = head_of(lax.rem(mine + GRP - t, GRP))

        @pl.when(t > 0)
        def _():
            state_copy(h, h).wait_recv()

        core = o0[h] + nn(gmat[h], sbuf[h])
        inv = lax.rsqrt(jnp.mean(core * core, axis=-1, keepdims=True) + 1e-6)
        nb[:, pl.ds(aligned(h * D, D), D)] = (core * inv * wgain[...]).astype(BF)
        for d in (2, 1, 3):
            ret_copy(d, h, d - 1).start()

    own_out = pltpu.make_async_copy(
        nb.at[my_rows, :], out.at[:, pl.ds(aligned(me * HV * D, HV * D), HV * D)], loc.at[0]
    )
    own_out.start()
    for d in (1, 3, 2):
        @pl.loop(0, HV)
        def _(h):
            ret_copy(d, h, d - 1).wait_recv()
    own_out.wait()

    for d in range(1, NH):
        for i in range(2):
            ab_copy(d, i).wait_send()

        @pl.loop(0, HK)
        def _(kh):
            for i in range(3):
                rows_copy(i, d, kh).wait_send()

        @pl.loop(0, HV)
        def _(h):
            ret_copy(d, h, d - 1).wait_send()

        @pl.when(yrow + d < nrow)
        def _():
            ya_copy(d).wait_send()

        @pl.when((yrow > 0) & (yrow + d < nrow))
        def _():
            yd_copy(d).wait_send()

    for i in range(3):
        halo_copy(i).wait_send()

    @pl.when(me == NH - 1)
    def _():
        for i in range(3):
            for d in range(1, NH):
                tail_copy(i, d).wait_send()

    @pl.loop(0, GRP)
    def _(i):
        @pl.when(i != my_head)
        def _():
            d_copy(i, mine).wait_send()
            a_copy(i, mine).wait_send()

        @pl.when(i != mine)
        def _():
            state_copy(i, my_head).wait_send()


def local(q, k, v, z, a, b, cq, ck, cv, alog, dtb, gain):
    any_spec = pl.BlockSpec(memory_space=pl.ANY)
    dma = pltpu.SemaphoreType.DMA

    def bf(*shape):
        return pltpu.VMEM(shape, BF)

    def f32(*shape):
        return pltpu.VMEM(shape, F32)

    scratch = dict(
        rq=bf(C, 512), rk=bf(C, 512), rv=bf(C, 1024), ra=bf(NH, 32, BLK), rb=bf(NH, 32, BLK),
        hq=bf(RIM, 512), hk=bf(RIM, 512), hv=bf(RIM, 1024), tq=bf(RIM, 512), tk=bf(RIM, 512), tv=bf(RIM, 1024), xs=f32(C + RIM, 256),
        wq=f32(4, 512), wk=f32(4, 512), wv=f32(4, 1024), walog=f32(1, HV), wdtb=f32(1, HV), wgain=f32(1, D),
        masks=bf(8, D, D), ccol=f32(HK, C, 4), crow=f32(HV, 1, C), brow=f32(HV, 1, C),
        dec=f32(HV, 3, D, D), nmat=bf(HV, 3, D, D), tmat=bf(HV, 2, D, D), ks=bf(HK, C, D), vs=bf(HK, C, 2 * D),
        kdt=bf(HV, D, C), mb=bf(HV, D, C), o0=f32(HV, C, D), gmat=bf(HV, C, D),
        dsend=bf(HV, D + 16, D), asend=bf(HV, D, D), dmap=bf(GRP, D + 16, D), amap=bf(GRP, D, D),
        pxd=bf(GRP, D, D), pxa=f32(GRP, D, D), pep=f32(GRP, 1, D), sfx=bf(D, (GRP - 1) * D), sfe=f32(GRP, 1, D),
        gds=bf(D + 16, D), gas=bf(D, D), gdm=bf(4, D + 16, D), gam=bf(4, D, D),
        state=f32(D, D), ssend=bf(GRP, D, D), sbuf=bf(HV, D, D), nb=bf(C, HV * D),
        k_s=dma((HK, 3)), k_r=dma((HK, 3)), v_s=dma((HK, 3)), v_r=dma((HK, 3)), q_s=dma((HK, 3)), q_r=dma((HK, 3)),
        ab_s=dma((3, 2)), ab_r=dma((3, 2)), tail_s=dma((3, 3)), tail_r=dma((3,)),
        halo_s=dma((3,)), halo_r=dma((3,)), loc=dma((11,)),
        d_s=dma((GRP,)), d_r=dma((GRP,)), a_s=dma((GRP,)), a_r=dma((GRP,)),
        yd_s=dma((3,)), yd_r=dma((4,)), ya_s=dma((3,)), ya_r=dma((4,)),
        st_s=dma((GRP,)), st_r=dma((GRP,)), ret_s=dma((HV, 3)), ret_r=dma((HV, 3)),
    )
    normed = pl.pallas_call(
        kernel,
        out_shape=jax.ShapeDtypeStruct((BLK, 4 * HV * D), BF),
        in_specs=[any_spec] * 11,
        out_specs=any_spec,
        scratch_shapes=list(scratch.values()),
        compiler_params=pltpu.CompilerParams(
            collective_id=0, has_side_effects=True, vmem_limit_bytes=67043328
        ),
    )(q, k, v, a.T, b.T, cq, ck, cv, alog.reshape(1, HV), dtb.reshape(1, HV), gain.reshape(1, D))
    return (normed.astype(F32) * jax.nn.silu(z.astype(F32))).astype(BF)


def solution(mesh):
    rows = P(("ctx", "head"), None)
    placed = (rows,) * 6 + (P(None, "head"),) * 3 + (P("head"), P("head"), P())
    return jax.shard_map(local, mesh=mesh, in_specs=placed, out_specs=rows, check_vma=False)
```

```python
import functools

import jax
import jax.numpy as jnp
from jax import lax
from jax.experimental import pallas as pl
from jax.experimental.pallas import tpu as pltpu
from jax.sharding import PartitionSpec as P

MESH = pl.DeviceIdType.MESH
F32 = jnp.float32
BF = jnp.bfloat16
HIGHEST = lax.Precision.HIGHEST

D = 128
BLK = 64
C = 256
HK = 4
HV = 8
NH = 4
GRP = 8
RIM = 8
NEG = -1e30


def nn(a, b, precision=None):
    return lax.dot_general(
        a, b, (((1,), (0,)), ((), ())), precision=precision, preferred_element_type=F32
    )


def nt(a, b):
    return lax.dot_general(a, b, (((1,), (1,)), ((), ())), preferred_element_type=F32)


def sigmoid(x):
    return 1.0 / (1.0 + jnp.exp(-x))


def remote(src, dst, send, recv, where):
    return pltpu.make_async_remote_copy(
        src_ref=src, dst_ref=dst, send_sem=send, recv_sem=recv, device_id=where, device_id_type=MESH
    )


def aligned(x, n):
    return pl.multiple_of(x, n)


def store_exact(ref, row):
    wide = jnp.broadcast_to(row, (16, D))
    e1 = wide.astype(BF).astype(F32)
    e2 = (wide - e1).astype(BF).astype(F32)
    e3 = wide - e1 - e2
    i = lax.broadcasted_iota(jnp.int32, (16, D), 0)
    ref[pl.ds(D, 16), :] = jnp.where(i == 0, e1, jnp.where(i == 1, e2, jnp.where(i == 2, e3, 0.0))).astype(BF)


def load_exact(ref):
    p = ref[pl.ds(D, 16), :].astype(F32)
    return p[0:1, :] + p[1:2, :] + p[2:3, :]


def times_inverse(lo, hi, t0, t1, n10):
    m1 = hi + nn(hi.astype(BF), t1)
    m = lo - nn(m1.astype(BF), n10)
    return m + nn(m.astype(BF), t0), m1


def kernel(
    q, k, v, a, b, cq, ck, cv, alog, dtb, gain,
    out,
    rq, rk, rv, ra, rb, hq, hk, hv, tq, tk, tv, xs, wq, wk, wv, walog, wdtb, wgain,
    masks, ccol, crow, brow, dec, nmat, tmat, ks, vs, kdt, mb, o0, gmat,
    dsend, asend, dmap, amap, pxd, pxa, pep, sfx, sfe, gds, gas, gdm, gam, state, ssend, sbuf, nb,
    k_s, k_r, v_s, v_r, q_s, q_r, ab_s, ab_r, tail_s, tail_r, halo_s, halo_r, loc,
    d_s, d_r, a_s, a_r, yd_s, yd_r, ya_s, ya_r, st_s, st_r, ret_s, ret_r,
):
    ctx = lax.axis_index("ctx")
    me = lax.axis_index("head")
    nctx = lax.axis_size("ctx")
    yrow = ctx // GRP
    base = yrow * GRP
    mine = ctx - base
    nrow = nctx // GRP
    prev = lax.rem(ctx + nctx - 1, nctx)
    nxt = lax.rem(ctx + 1, nctx)

    def owner(h):
        return lax.rem(h, 4) * 2 + h // 4

    def head_of(m):
        return lax.rem(m, 2) * 4 + m // 2

    my_head = head_of(mine)

    def peer(d):
        return lax.rem(me + d, NH)

    def source(d):
        return lax.rem(me + NH - d, NH)

    KINDS = (
        (k, rk, hk, tk, 512, D, k_s, k_r),
        (v, rv, hv, tv, 1024, 2 * D, v_s, v_r),
        (q, rq, hq, tq, 512, D, q_s, q_r),
    )
    my_rows = pl.ds(aligned(me * BLK, BLK), BLK)

    def own_copies():
        cps = []
        for i, (src, dst) in enumerate(
            ((ck, wk), (cv, wv), (cq, wq), (alog, walog), (dtb, wdtb), (gain, wgain), (a, ra.at[me]), (b, rb.at[me]))
        ):
            cps.append(pltpu.make_async_copy(src, dst, loc.at[i]))
        for i, (src, dst, _, _, w, _, _, _) in enumerate(KINDS):
            cps.append(pltpu.make_async_copy(src.at[:, pl.ds(aligned(me * w, w), w)], dst.at[my_rows, :], loc.at[8 + i]))
        return cps

    for cp in own_copies():
        cp.start()

    barrier = pltpu.get_barrier_semaphore()
    for d in range(1, NH):
        pl.semaphore_signal(barrier, inc=1, device_id={"head": peer(d)}, device_id_type=MESH)
    for d in range(1, GRP):
        pl.semaphore_signal(barrier, inc=1, device_id={"ctx": base + lax.rem(mine + d, GRP)}, device_id_type=MESH)
    for d in range(1, 4):
        pl.semaphore_signal(barrier, inc=1, device_id={"ctx": lax.rem(ctx + d * GRP, nctx)}, device_id_type=MESH)

    for near in (prev, nxt):
        pl.semaphore_signal(barrier, inc=1, device_id={"ctx": near}, device_id_type=MESH)
    r1 = lax.broadcasted_iota(jnp.int32, (D, D), 0)
    c1 = lax.broadcasted_iota(jnp.int32, (D, D), 1)
    gap = r1 ^ c1
    masks[0] = (r1 == c1).astype(F32).astype(BF)
    for i in range(7):
        masks[i + 1] = jnp.where((gap >= 2**i) & (gap < 2 ** (i + 1)) & (r1 > c1), -1.0, 0.0).astype(BF)
    pl.semaphore_wait(barrier, 3 + 7 + 3 + 2)

    def ab_copy(d, i):
        src, dst = ((a, ra), (b, rb))[i]
        return remote(src, dst.at[me], ab_s.at[d - 1, i], ab_r.at[d - 1, i], {"head": peer(d)})

    def rows_copy(i, d, kh):
        src, dst, _, _, w, cw, ssem, rsem = KINDS[i]
        return remote(
            src.at[:, pl.ds(aligned(peer(d) * w + kh * cw, cw), cw)],
            dst.at[my_rows, pl.ds(aligned(kh * cw, cw), cw)],
            ssem.at[kh, d - 1], rsem.at[kh, d - 1], {"head": peer(d)},
        )

    def tail_copy(i, d):
        src, _, _, dst, w, _, _, _ = KINDS[i]
        return remote(
            src.at[pl.ds(BLK - RIM, RIM), pl.ds(aligned(peer(d) * w, w), w)], dst, tail_s.at[i, d - 1], tail_r.at[i],
            {"head": peer(d)},
        )

    def halo_copy(i):
        _, _, dst, src, _, _, _, _ = KINDS[i]
        return remote(src, dst, halo_s.at[i], halo_r.at[i], {"ctx": nxt})

    def halo_first(i):
        src, _, dst, _, w, _, _, _ = KINDS[i]
        return remote(
            src.at[pl.ds(BLK - RIM, RIM), pl.ds((NH - 1) * w, w)], dst, halo_s.at[i], halo_r.at[i], {"ctx": nxt}
        )

    def send_tails(*kinds):
        @pl.when(me == NH - 1)
        def _():
            for i in kinds:
                for d in (2, 1, 3):
                    tail_copy(i, d).start()
            for i in kinds:
                halo_first(i).start()

    def pass_tails(*kinds):
        @pl.when(me < NH - 1)
        def _():
            for i in kinds:
                tail_copy(i, 1).wait_recv()
                halo_copy(i).start()

    for d in (2, 1, 3):
        for i in range(2):
            ab_copy(d, i).start()
    send_tails(0, 1, 2)
    for i in range(3):
        @pl.loop(0, HK)
        def _(kh):
            for d in (2, 1, 3):
                rows_copy(i, d, kh).start()

        if i == 0:
            pass_tails(0, 1, 2)

    for cp in own_copies():
        cp.wait()
    for d in range(1, NH):
        for i in range(2):
            ab_copy(d, i).wait_recv()
    sel = (
        lax.broadcasted_iota(jnp.int32, (HV, 32), 1) == lax.broadcasted_iota(jnp.int32, (HV, 32), 0) + me * HV
    ).astype(F32).astype(BF)
    eye8 = lax.broadcasted_iota(jnp.int32, (HV, HV), 0) == lax.broadcasted_iota(jnp.int32, (HV, HV), 1)

    def column(row):
        return jnp.sum(jnp.where(eye8, jnp.broadcast_to(row, (HV, HV)), 0.0), axis=1, keepdims=True)

    a_row = jnp.concatenate([nn(sel, ra[s]) for s in range(NH)], axis=1) + column(wdtb[...])
    b_row = jnp.concatenate([nn(sel, rb[s]) for s in range(NH)], axis=1)
    g_row = -column(jnp.exp(walog[...])) * (jnp.maximum(a_row, 0.0) + jnp.log1p(jnp.exp(-jnp.abs(a_row))))
    beta_row = sigmoid(b_row)
    row = lax.broadcasted_iota(jnp.int32, (C, C), 0)
    col = lax.broadcasted_iota(jnp.int32, (C, C), 1)
    c_row = nn(g_row, (row <= col).astype(F32), HIGHEST)
    both = jnp.transpose(jnp.concatenate([c_row, beta_row], axis=0))
    for kh in range(HK):
        ccol[kh, :, 0:2] = both[:, 2 * kh : 2 * kh + 2]
        ccol[kh, :, 2:4] = both[:, HV + 2 * kh : HV + 2 * kh + 2]
    for h in range(HV):
        crow[h] = c_row[h : h + 1, :]
        brow[h] = beta_row[h : h + 1, :]
    inside = jnp.where(ctx > 0, 1.0, 0.0).astype(F32)

    def arrived(i, kh):
        for d in range(1, NH):
            rows_copy(i, d, kh).wait_recv()

    def conv_silu(i, taps, kh):
        _, rows, halo, _, _, cw, _, _ = KINDS[i]
        cols = pl.ds(aligned(kh * cw, cw), cw)
        here = pl.ds(0, cw)
        xs[pl.ds(0, RIM), here] = halo[:, cols].astype(F32) * inside
        xs[pl.ds(RIM, C), here] = rows[:, cols].astype(F32)
        w = taps[:, cols]
        total = w[0:1, :] * xs[pl.ds(RIM - 3, C), here]
        for j in range(1, 4):
            total = total + w[j : j + 1, :] * xs[pl.ds(RIM - 3 + j, C), here]
        return total * sigmoid(total)

    def unit(x, factor):
        return (x * (lax.rsqrt(jnp.sum(x * x, axis=-1, keepdims=True) + 1e-6) * factor)).astype(BF)

    halo_copy(0).wait_recv()

    def key_head(kh):
        arrived(0, kh)
        kn = unit(conv_silu(0, wk, kh), 1.0)
        ks[kh] = kn
        kt = jnp.transpose(kn.astype(F32))
        kk00, kk1 = nt(kn[:D], kn[:D]), nt(kn[D:], kn)
        cc = ccol[kh]
        low = lax.broadcasted_iota(jnp.int32, (D, D), 0) >= lax.broadcasted_iota(jnp.int32, (D, D), 1)
        for j in range(2):
            h = 2 * kh + j
            cj, bj, cr = cc[:, j : j + 1], cc[:, 2 + j : 3 + j], crow[h]
            d00 = jnp.exp(jnp.where(low, cj[:D] - cr[:, :D], NEG))
            d10 = jnp.exp(cj[D:] - cr[:, :D])
            d11 = jnp.exp(jnp.where(low, cj[D:] - cr[:, D:], NEG))
            dec[h, 0], dec[h, 1], dec[h, 2] = d00, d10, d11
            nmat[h, 0] = (bj[:D] * d00 * kk00).astype(BF)
            nmat[h, 1] = (bj[D:] * d10 * kk1[:, :D]).astype(BF)
            nmat[h, 2] = (bj[D:] * d11 * kk1[:, D:]).astype(BF)
            kdt[h] = (kt * jnp.exp(cr[:, C - 1 : C] - cr)).astype(BF)

    def d_copy(h, slot):
        return remote(dsend.at[h], dmap.at[mine], d_s.at[h], d_r.at[slot], {"ctx": base + owner(h)})

    def a_copy(h, slot):
        return remote(asend.at[h], amap.at[mine], a_s.at[h], a_r.at[slot], {"ctx": base + owner(h)})

    def hand_over(copy, kept, sent, h):
        @pl.when(h != my_head)
        def _():
            copy(h, mine).start()

        @pl.when(h == my_head)
        def _():
            kept[mine] = sent[h]

    @pl.loop(0, 2)
    def _(half):
        pl.loop(2 * half, 2 * half + 2)(key_head)

        heads = [4 * half + x for x in range(4)]
        chains = [(h, i) for h in heads for i in (0, 2)]
        ts = [masks[0] + nmat[h, i] * masks[1] for h, i in chains]
        for level in range(2, 8):
            left = [nn(t, nmat[h, i] * masks[level]).astype(BF) for t, (h, i) in zip(ts, chains)]
            ts = [t + nn(x, t).astype(BF) for t, x in zip(ts, left)]
        for t, (h, i) in zip(ts, chains):
            tmat[h, i // 2] = t - masks[0]

        m1 = [kdt[h, :, D:].astype(F32) + nn(kdt[h, :, D:], tmat[h, 1]) for h in heads]
        m0 = [kdt[h, :, :D].astype(F32) - nn(x.astype(BF), nmat[h, 1]) for x, h in zip(m1, heads)]
        m0 = [x + nn(x.astype(BF), tmat[h, 0]) for x, h in zip(m0, heads)]
        for x, h in enumerate(heads):
            cr = crow[h]
            m = jnp.concatenate([m0[x], m1[x]], axis=1) * brow[h]
            mb[h] = m.astype(BF)
            dsend[h, pl.ds(0, D), :] = (-nn((m * jnp.exp(cr)).astype(BF), ks[2 * half + x // 2])).astype(BF)
            store_exact(dsend.at[h], jnp.broadcast_to(jnp.exp(cr[:, C - 1 : C]), (1, D)))
        for h in heads:
            hand_over(d_copy, dmap, dsend, h)

    halo_copy(1).wait_recv()

    @pl.loop(0, HK)
    def _(kh):
        arrived(1, kh)
        vn = conv_silu(1, wv, kh).astype(BF)
        vs[kh] = vn
        for j in range(2):
            h = 2 * kh + j
            asend[h] = nn(mb[h], vn[:, j * D : (j + 1) * D]).astype(BF)
        for j in range(2):
            hand_over(a_copy, amap, asend, 2 * kh + j)

    halo_copy(2).wait_recv()

    def own_tokens(pair):
        for kh in (2 * pair, 2 * pair + 1):
            arrived(2, kh)
        qn = [unit(conv_silu(2, wq, kh), D ** -0.5) for kh in (2 * pair, 2 * pair + 1)]
        todo = []
        for g in range(2):
            kh = 2 * pair + g
            kn = ks[kh]
            qk00, qk1 = nt(qn[g][:D], kn[:D]), nt(qn[g][D:], kn)
            for j in range(2):
                h = 2 * kh + j
                todo.append((kh, j, h, g, dec[h, 0] * qk00, dec[h, 1] * qk1[:, :D], dec[h, 2] * qk1[:, D:]))
        m1 = [hi + nn(hi.astype(BF), tmat[h, 1]) for _, _, h, _, _, _, hi in todo]
        m0 = [lo - nn(x.astype(BF), nmat[h, 1]) for x, (_, _, h, _, _, lo, _) in zip(m1, todo)]
        p00 = [top + nn(top.astype(BF), tmat[h, 0]) for _, _, h, _, top, _, _ in todo]
        m0 = [x + nn(x.astype(BF), tmat[h, 0]) for x, (_, _, h, _, _, _, _) in zip(m0, todo)]
        for n, (kh, j, h, g, _, _, _) in enumerate(todo):
            grow = jnp.exp(ccol[kh][:, j : j + 1])
            bt = brow[h]
            btg = bt * jnp.exp(crow[h])
            kn, vj, qf = ks[kh], vs[kh][:, j * D : (j + 1) * D], qn[g].astype(F32)
            p1 = jnp.concatenate([m0[n], m1[n]], axis=1)
            o0[h, pl.ds(0, D), :] = nn((p00[n] * bt[:, :D]).astype(BF), vj[:D])
            o0[h, pl.ds(D, D), :] = nn((p1 * bt).astype(BF), vj)
            gmat[h, pl.ds(0, D), :] = (grow[:D] * qf[:D] - nn((p00[n] * btg[:, :D]).astype(BF), kn[:D])).astype(BF)
            gmat[h, pl.ds(D, D), :] = (grow[D:] * qf[D:] - nn((p1 * btg).astype(BF), kn)).astype(BF)

    own_tokens(0)

    def wait_from(copy, i):
        @pl.when(mine != i)
        def _():
            copy(i, i).wait_recv()

    for i in range(GRP):
        wait_from(d_copy, i)
    lin = [dmap[i, pl.ds(0, D), :] for i in range(GRP)]
    decays = [load_exact(dmap.at[i]) for i in range(GRP)]
    xd, ep = lin[0].astype(F32), decays[0]
    sd, es = lin[GRP - 1].astype(F32), decays[GRP - 1]
    pxd[0] = jnp.zeros((D, D), BF)
    pep[0] = jnp.ones((1, D), F32)
    for i in range(1, GRP):
        xb = xd.astype(BF)
        pxd[i] = xb
        pep[i] = ep
        xd = decays[i] * xd + nn(lin[i], xb) + ep * lin[i].astype(F32)
        ep = ep * decays[i]
        m = GRP - 1 - i
        sb = sd.astype(BF)
        sfx[:, m * D : (m + 1) * D] = sb
        sfe[m] = es
        if m > 0:
            sd = decays[m] * sd + nn(sb, lin[m]) + es * lin[m].astype(F32)
            es = es * decays[m]
    gds[pl.ds(0, D), :] = xd.astype(BF)
    store_exact(gds, ep)

    def yd_copy(d):
        return remote(gds, gdm.at[yrow], yd_s.at[d - 1], yd_r.at[yrow], {"ctx": lax.rem(ctx + d * GRP, nctx)})

    def ya_copy(d):
        return remote(gas, gam.at[yrow], ya_s.at[d - 1], ya_r.at[yrow], {"ctx": lax.rem(ctx + d * GRP, nctx)})

    for d in range(1, 4):
        @pl.when((yrow > 0) & (yrow + d < nrow))
        def _():
            yd_copy(d).start()

    for i in range(GRP):
        wait_from(a_copy, i)
    add = [amap[i] for i in range(GRP)]
    total = add[GRP - 1].astype(F32) + nn(sfx[...], jnp.concatenate(add[: GRP - 1], axis=0))
    for i in range(GRP - 1):
        total = total + sfe[i] * add[i].astype(F32)
    gas[...] = total.astype(BF)
    for d in range(1, 4):
        @pl.when(yrow + d < nrow)
        def _():
            ya_copy(d).start()

    xa = add[0].astype(F32)
    pxa[0] = jnp.zeros((D, D), F32)
    for i in range(1, GRP):
        pxa[i] = xa
        if i < GRP - 1:
            xa = decays[i] * xa + nn(lin[i], xa.astype(BF)) + add[i].astype(F32)
    own_tokens(1)

    state[...] = jnp.zeros_like(state)
    for yy in range(3):
        @pl.when(yy < yrow)
        def _():
            remote(gas, gam.at[yy], ya_s.at[0], ya_r.at[yy], {"ctx": prev}).wait_recv()
            if yy == 0:
                state[...] = gam[0].astype(F32)
            else:
                remote(gds, gdm.at[yy], yd_s.at[0], yd_r.at[yy], {"ctx": prev}).wait_recv()
                s_now = state[...]
                state[...] = (
                    load_exact(gdm.at[yy]) * s_now
                    + nn(gdm[yy, pl.ds(0, D), :], s_now.astype(BF))
                    + gam[yy].astype(F32)
                )

    def state_copy(i, slot):
        return remote(ssend.at[i], sbuf.at[my_head], st_s.at[i], st_r.at[slot], {"ctx": base + i})

    s_in = state[...]
    moved = nn(jnp.concatenate([pxd[i] for i in range(GRP)], axis=0), s_in.astype(BF))
    for i in range(GRP):
        ssend[i] = (pep[i] * s_in + moved[i * D : (i + 1) * D] + pxa[i]).astype(BF)
    for t in range(1, GRP):
        state_copy(lax.rem(mine + t, GRP), my_head).start()
    sbuf[my_head] = ssend[mine]

    def ret_copy(d, h, slot):
        return remote(
            nb.at[pl.ds(aligned(peer(d) * BLK, BLK), BLK), pl.ds(aligned(h * D, D), D)],
            out.at[:, pl.ds(aligned(me * HV * D + h * D, D), D)],
            ret_s.at[h, d - 1], ret_r.at[h, slot], {"head": peer(d)},
        )

    @pl.loop(0, GRP)
    def _(t):
        h = head_of(lax.rem(mine + GRP - t, GRP))

        @pl.when(t > 0)
        def _():
            state_copy(h, h).wait_recv()

        core = o0[h] + nn(gmat[h], sbuf[h])
        inv = lax.rsqrt(jnp.mean(core * core, axis=-1, keepdims=True) + 1e-6)
        nb[:, pl.ds(aligned(h * D, D), D)] = (core * inv * wgain[...]).astype(BF)
        for d in (2, 1, 3):
            ret_copy(d, h, d - 1).start()

    own_out = pltpu.make_async_copy(
        nb.at[my_rows, :], out.at[:, pl.ds(aligned(me * HV * D, HV * D), HV * D)], loc.at[0]
    )
    own_out.start()
    for d in (1, 3, 2):
        @pl.loop(0, HV)
        def _(h):
            ret_copy(d, h, d - 1).wait_recv()
    own_out.wait()

    for d in range(1, NH):
        for i in range(2):
            ab_copy(d, i).wait_send()

        @pl.loop(0, HK)
        def _(kh):
            for i in range(3):
                rows_copy(i, d, kh).wait_send()

        @pl.loop(0, HV)
        def _(h):
            ret_copy(d, h, d - 1).wait_send()

        @pl.when(yrow + d < nrow)
        def _():
            ya_copy(d).wait_send()

        @pl.when((yrow > 0) & (yrow + d < nrow))
        def _():
            yd_copy(d).wait_send()

    for i in range(3):
        halo_copy(i).wait_send()

    @pl.when(me == NH - 1)
    def _():
        for i in range(3):
            for d in range(1, NH):
                tail_copy(i, d).wait_send()

    @pl.loop(0, GRP)
    def _(i):
        @pl.when(i != my_head)
        def _():
            d_copy(i, mine).wait_send()
            a_copy(i, mine).wait_send()

        @pl.when(i != mine)
        def _():
            state_copy(i, my_head).wait_send()


def local(q, k, v, z, a, b, cq, ck, cv, alog, dtb, gain):
    any_spec = pl.BlockSpec(memory_space=pl.ANY)
    dma = pltpu.SemaphoreType.DMA

    def bf(*shape):
        return pltpu.VMEM(shape, BF)

    def f32(*shape):
        return pltpu.VMEM(shape, F32)

    scratch = dict(
        rq=bf(C, 512), rk=bf(C, 512), rv=bf(C, 1024), ra=bf(NH, 32, BLK), rb=bf(NH, 32, BLK),
        hq=bf(RIM, 512), hk=bf(RIM, 512), hv=bf(RIM, 1024), tq=bf(RIM, 512), tk=bf(RIM, 512), tv=bf(RIM, 1024), xs=f32(C + RIM, 256),
        wq=f32(4, 512), wk=f32(4, 512), wv=f32(4, 1024), walog=f32(1, HV), wdtb=f32(1, HV), wgain=f32(1, D),
        masks=bf(8, D, D), ccol=f32(HK, C, 4), crow=f32(HV, 1, C), brow=f32(HV, 1, C),
        dec=f32(HV, 3, D, D), nmat=bf(HV, 3, D, D), tmat=bf(HV, 2, D, D), ks=bf(HK, C, D), vs=bf(HK, C, 2 * D),
        kdt=bf(HV, D, C), mb=bf(HV, D, C), o0=f32(HV, C, D), gmat=bf(HV, C, D),
        dsend=bf(HV, D + 16, D), asend=bf(HV, D, D), dmap=bf(GRP, D + 16, D), amap=bf(GRP, D, D),
        pxd=bf(GRP, D, D), pxa=f32(GRP, D, D), pep=f32(GRP, 1, D), sfx=bf(D, (GRP - 1) * D), sfe=f32(GRP, 1, D),
        gds=bf(D + 16, D), gas=bf(D, D), gdm=bf(4, D + 16, D), gam=bf(4, D, D),
        state=f32(D, D), ssend=bf(GRP, D, D), sbuf=bf(HV, D, D), nb=bf(C, HV * D),
        k_s=dma((HK, 3)), k_r=dma((HK, 3)), v_s=dma((HK, 3)), v_r=dma((HK, 3)), q_s=dma((HK, 3)), q_r=dma((HK, 3)),
        ab_s=dma((3, 2)), ab_r=dma((3, 2)), tail_s=dma((3, 3)), tail_r=dma((3,)),
        halo_s=dma((3,)), halo_r=dma((3,)), loc=dma((11,)),
        d_s=dma((GRP,)), d_r=dma((GRP,)), a_s=dma((GRP,)), a_r=dma((GRP,)),
        yd_s=dma((3,)), yd_r=dma((4,)), ya_s=dma((3,)), ya_r=dma((4,)),
        st_s=dma((GRP,)), st_r=dma((GRP,)), ret_s=dma((HV, 3)), ret_r=dma((HV, 3)),
    )
    normed = pl.pallas_call(
        kernel,
        out_shape=pltpu.VMEM((BLK, 4 * HV * D), BF),
        in_specs=[any_spec] * 11,
        out_specs=any_spec,
        scratch_shapes=list(scratch.values()),
        compiler_params=pltpu.CompilerParams(
            collective_id=0, has_side_effects=True, vmem_limit_bytes=60 * 1024 * 1024
        ),
    )(q, k, v, a.T, b.T, cq, ck, cv, alog.reshape(1, HV), dtb.reshape(1, HV), gain.reshape(1, D))
    return (normed.astype(F32) * jax.nn.silu(z.astype(F32))).astype(BF)


def solution(mesh):
    rows = P(("ctx", "head"), None)
    placed = (rows,) * 6 + (P(None, "head"),) * 3 + (P("head"), P("head"), P())
    return jax.shard_map(local, mesh=mesh, in_specs=placed, out_specs=rows, check_vma=False)
```

```python
import functools

import jax
import jax.numpy as jnp
from jax import lax
from jax.experimental import pallas as pl
from jax.experimental.pallas import tpu as pltpu
from jax.sharding import PartitionSpec as P

MESH = pl.DeviceIdType.MESH
F32 = jnp.float32
BF = jnp.bfloat16
HIGHEST = lax.Precision.HIGHEST

D = 128
BLK = 64
C = 256
HK = 4
HV = 8
NH = 4
GRP = 8
RIM = 8
NEG = -1e30


def nn(a, b, precision=None):
    return lax.dot_general(
        a, b, (((1,), (0,)), ((), ())), precision=precision, preferred_element_type=F32
    )


def nt(a, b):
    return lax.dot_general(a, b, (((1,), (1,)), ((), ())), preferred_element_type=F32)


def sigmoid(x):
    return 1.0 / (1.0 + jnp.exp(-x))


def remote(src, dst, send, recv, where):
    return pltpu.make_async_remote_copy(
        src_ref=src, dst_ref=dst, send_sem=send, recv_sem=recv, device_id=where, device_id_type=MESH
    )


def aligned(x, n):
    return pl.multiple_of(x, n)


def store_exact(ref, row):
    wide = jnp.broadcast_to(row, (16, D))
    e1 = wide.astype(BF).astype(F32)
    e2 = (wide - e1).astype(BF).astype(F32)
    e3 = wide - e1 - e2
    i = lax.broadcasted_iota(jnp.int32, (16, D), 0)
    ref[pl.ds(D, 16), :] = jnp.where(i == 0, e1, jnp.where(i == 1, e2, jnp.where(i == 2, e3, 0.0))).astype(BF)


def load_exact(ref):
    p = ref[pl.ds(D, 16), :].astype(F32)
    return p[0:1, :] + p[1:2, :] + p[2:3, :]


def times_inverse(lo, hi, t0, t1, n10):
    m1 = hi + nn(hi.astype(BF), t1)
    m = lo - nn(m1.astype(BF), n10)
    return m + nn(m.astype(BF), t0), m1


def kernel(
    q, k, v, a, b, cq, ck, cv, alog, dtb, gain,
    out,
    rq, rk, rv, ra, rb, hq, hk, hv, tq, tk, tv, xs, wq, wk, wv, walog, wdtb, wgain,
    masks, ccol, crow, brow, dec, nmat, tmat, ks, vs, kdt, mb, o0, gmat,
    dsend, asend, dmap, amap, pxd, pxa, pep, sfx, sfe, gds, gas, gdm, gam, state, ssend, sbuf, nb,
    k_s, k_r, v_s, v_r, q_s, q_r, ab_s, ab_r, tail_s, tail_r, halo_s, halo_r, loc,
    d_s, d_r, a_s, a_r, yd_s, yd_r, ya_s, ya_r, st_s, st_r, ret_s, ret_r,
):
    ctx = lax.axis_index("ctx")
    me = lax.axis_index("head")
    nctx = lax.axis_size("ctx")
    yrow = ctx // GRP
    base = yrow * GRP
    mine = ctx - base
    nrow = nctx // GRP
    prev = lax.rem(ctx + nctx - 1, nctx)
    nxt = lax.rem(ctx + 1, nctx)

    def owner(h):
        return lax.rem(h, 4) * 2 + h // 4

    def head_of(m):
        return lax.rem(m, 2) * 4 + m // 2

    my_head = head_of(mine)

    def peer(d):
        return lax.rem(me + d, NH)

    def source(d):
        return lax.rem(me + NH - d, NH)

    KINDS = (
        (k, rk, hk, tk, 512, D, k_s, k_r),
        (v, rv, hv, tv, 1024, 2 * D, v_s, v_r),
        (q, rq, hq, tq, 512, D, q_s, q_r),
    )
    my_rows = pl.ds(aligned(me * BLK, BLK), BLK)

    def own_copies():
        cps = []
        for i, (src, dst) in enumerate(
            ((ck, wk), (cv, wv), (cq, wq), (alog, walog), (dtb, wdtb), (gain, wgain), (a, ra.at[me]), (b, rb.at[me]))
        ):
            cps.append(pltpu.make_async_copy(src, dst, loc.at[i]))
        for i, (src, dst, _, _, w, _, _, _) in enumerate(KINDS):
            cps.append(pltpu.make_async_copy(src.at[:, pl.ds(aligned(me * w, w), w)], dst.at[my_rows, :], loc.at[8 + i]))
        return cps

    for cp in own_copies():
        cp.start()

    barrier = pltpu.get_barrier_semaphore()
    for d in range(1, NH):
        pl.semaphore_signal(barrier, inc=1, device_id={"head": peer(d)}, device_id_type=MESH)
    for d in range(1, GRP):
        pl.semaphore_signal(barrier, inc=1, device_id={"ctx": base + lax.rem(mine + d, GRP)}, device_id_type=MESH)
    for d in range(1, 4):
        pl.semaphore_signal(barrier, inc=1, device_id={"ctx": lax.rem(ctx + d * GRP, nctx)}, device_id_type=MESH)

    for near in (prev, nxt):
        pl.semaphore_signal(barrier, inc=1, device_id={"ctx": near}, device_id_type=MESH)
    r1 = lax.broadcasted_iota(jnp.int32, (D, D), 0)
    c1 = lax.broadcasted_iota(jnp.int32, (D, D), 1)
    gap = r1 ^ c1
    masks[0] = (r1 == c1).astype(F32).astype(BF)
    for i in range(7):
        masks[i + 1] = jnp.where((gap >= 2**i) & (gap < 2 ** (i + 1)) & (r1 > c1), -1.0, 0.0).astype(BF)
    pl.semaphore_wait(barrier, 3 + 7 + 3 + 2)

    def ab_copy(d, i):
        src, dst = ((a, ra), (b, rb))[i]
        return remote(src, dst.at[me], ab_s.at[d - 1, i], ab_r.at[d - 1, i], {"head": peer(d)})

    def rows_copy(i, d, kh):
        src, dst, _, _, w, cw, ssem, rsem = KINDS[i]
        return remote(
            src.at[:, pl.ds(aligned(peer(d) * w + kh * cw, cw), cw)],
            dst.at[my_rows, pl.ds(aligned(kh * cw, cw), cw)],
            ssem.at[kh, d - 1], rsem.at[kh, d - 1], {"head": peer(d)},
        )

    def tail_copy(i, d):
        src, _, _, dst, w, _, _, _ = KINDS[i]
        return remote(
            src.at[pl.ds(BLK - RIM, RIM), pl.ds(aligned(peer(d) * w, w), w)], dst, tail_s.at[i, d - 1], tail_r.at[i],
            {"head": peer(d)},
        )

    def halo_copy(i):
        _, _, dst, src, _, _, _, _ = KINDS[i]
        return remote(src, dst, halo_s.at[i], halo_r.at[i], {"ctx": nxt})

    def halo_first(i):
        src, _, dst, _, w, _, _, _ = KINDS[i]
        return remote(
            src.at[pl.ds(BLK - RIM, RIM), pl.ds((NH - 1) * w, w)], dst, halo_s.at[i], halo_r.at[i], {"ctx": nxt}
        )

    def send_tails(*kinds):
        @pl.when(me == NH - 1)
        def _():
            for i in kinds:
                for d in (2, 1, 3):
                    tail_copy(i, d).start()
            for i in kinds:
                halo_first(i).start()

    def pass_tails(*kinds):
        @pl.when(me < NH - 1)
        def _():
            for i in kinds:
                tail_copy(i, 1).wait_recv()
                halo_copy(i).start()

    send_tails(0)
    for d in (2, 1, 3):
        for i in range(2):
            ab_copy(d, i).start()
    send_tails(1, 2)
    for i in range(3):
        @pl.loop(1 if i == 1 else 0, HK)
        def _(kh):
            for d in (2, 1, 3):
                rows_copy(i, d, kh).start()

        if i == 0:
            for d in (2, 1, 3):
                rows_copy(1, d, 0).start()
            pass_tails(0, 1, 2)

    for cp in own_copies():
        cp.wait()
    for d in range(1, NH):
        for i in range(2):
            ab_copy(d, i).wait_recv()
    sel = (
        lax.broadcasted_iota(jnp.int32, (HV, 32), 1) == lax.broadcasted_iota(jnp.int32, (HV, 32), 0) + me * HV
    ).astype(F32).astype(BF)
    eye8 = lax.broadcasted_iota(jnp.int32, (HV, HV), 0) == lax.broadcasted_iota(jnp.int32, (HV, HV), 1)

    def column(row):
        return jnp.sum(jnp.where(eye8, jnp.broadcast_to(row, (HV, HV)), 0.0), axis=1, keepdims=True)

    a_row = jnp.concatenate([nn(sel, ra[s]) for s in range(NH)], axis=1) + column(wdtb[...])
    b_row = jnp.concatenate([nn(sel, rb[s]) for s in range(NH)], axis=1)
    g_row = -column(jnp.exp(walog[...])) * (jnp.maximum(a_row, 0.0) + jnp.log1p(jnp.exp(-jnp.abs(a_row))))
    beta_row = sigmoid(b_row)
    row = lax.broadcasted_iota(jnp.int32, (C, C), 0)
    col = lax.broadcasted_iota(jnp.int32, (C, C), 1)
    c_row = nn(g_row, (row <= col).astype(F32), HIGHEST)
    both = jnp.transpose(jnp.concatenate([c_row, beta_row], axis=0))
    for kh in range(HK):
        ccol[kh, :, 0:2] = both[:, 2 * kh : 2 * kh + 2]
        ccol[kh, :, 2:4] = both[:, HV + 2 * kh : HV + 2 * kh + 2]
    for h in range(HV):
        crow[h] = c_row[h : h + 1, :]
        brow[h] = beta_row[h : h + 1, :]
    inside = jnp.where(ctx > 0, 1.0, 0.0).astype(F32)

    def arrived(i, kh):
        for d in range(1, NH):
            rows_copy(i, d, kh).wait_recv()

    def conv_silu(i, taps, kh):
        _, rows, halo, _, _, cw, _, _ = KINDS[i]
        cols = pl.ds(aligned(kh * cw, cw), cw)
        here = pl.ds(0, cw)
        xs[pl.ds(0, RIM), here] = halo[:, cols].astype(F32) * inside
        xs[pl.ds(RIM, C), here] = rows[:, cols].astype(F32)
        w = taps[:, cols]
        total = w[0:1, :] * xs[pl.ds(RIM - 3, C), here]
        for j in range(1, 4):
            total = total + w[j : j + 1, :] * xs[pl.ds(RIM - 3 + j, C), here]
        return total * sigmoid(total)

    def unit(x, factor):
        return (x * (lax.rsqrt(jnp.sum(x * x, axis=-1, keepdims=True) + 1e-6) * factor)).astype(BF)

    halo_copy(0).wait_recv()

    def key_head(kh):
        arrived(0, kh)
        kn = unit(conv_silu(0, wk, kh), 1.0)
        ks[kh] = kn
        kt = jnp.transpose(kn.astype(F32))
        kk00, kk1 = nt(kn[:D], kn[:D]), nt(kn[D:], kn)
        cc = ccol[kh]
        low = lax.broadcasted_iota(jnp.int32, (D, D), 0) >= lax.broadcasted_iota(jnp.int32, (D, D), 1)
        for j in range(2):
            h = 2 * kh + j
            cj, bj, cr = cc[:, j : j + 1], cc[:, 2 + j : 3 + j], crow[h]
            d00 = jnp.exp(jnp.where(low, cj[:D] - cr[:, :D], NEG))
            d10 = jnp.exp(cj[D:] - cr[:, :D])
            d11 = jnp.exp(jnp.where(low, cj[D:] - cr[:, D:], NEG))
            dec[h, 0], dec[h, 1], dec[h, 2] = d00, d10, d11
            nmat[h, 0] = (bj[:D] * d00 * kk00).astype(BF)
            nmat[h, 1] = (bj[D:] * d10 * kk1[:, :D]).astype(BF)
            nmat[h, 2] = (bj[D:] * d11 * kk1[:, D:]).astype(BF)
            kdt[h] = (kt * jnp.exp(cr[:, C - 1 : C] - cr)).astype(BF)

    def d_copy(h, slot):
        return remote(dsend.at[h], dmap.at[mine], d_s.at[h], d_r.at[slot], {"ctx": base + owner(h)})

    def a_copy(h, slot):
        return remote(asend.at[h], amap.at[mine], a_s.at[h], a_r.at[slot], {"ctx": base + owner(h)})

    def hand_over(copy, kept, sent, h):
        @pl.when(h != my_head)
        def _():
            copy(h, mine).start()

        @pl.when(h == my_head)
        def _():
            kept[mine] = sent[h]

    @pl.loop(0, 2)
    def _(half):
        pl.loop(2 * half, 2 * half + 2)(key_head)

        heads = [4 * half + x for x in range(4)]
        chains = [(h, i) for h in heads for i in (0, 2)]
        ts = [masks[0] + nmat[h, i] * masks[1] for h, i in chains]
        for level in range(2, 8):
            left = [nn(t, nmat[h, i] * masks[level]).astype(BF) for t, (h, i) in zip(ts, chains)]
            ts = [t + nn(x, t).astype(BF) for t, x in zip(ts, left)]
        for t, (h, i) in zip(ts, chains):
            tmat[h, i // 2] = t - masks[0]

        m1 = [kdt[h, :, D:].astype(F32) + nn(kdt[h, :, D:], tmat[h, 1]) for h in heads]
        m0 = [kdt[h, :, :D].astype(F32) - nn(x.astype(BF), nmat[h, 1]) for x, h in zip(m1, heads)]
        m0 = [x + nn(x.astype(BF), tmat[h, 0]) for x, h in zip(m0, heads)]
        for x, h in enumerate(heads):
            cr = crow[h]
            m = jnp.concatenate([m0[x], m1[x]], axis=1) * brow[h]
            mb[h] = m.astype(BF)
            dsend[h, pl.ds(0, D), :] = (-nn((m * jnp.exp(cr)).astype(BF), ks[2 * half + x // 2])).astype(BF)
            store_exact(dsend.at[h], jnp.broadcast_to(jnp.exp(cr[:, C - 1 : C]), (1, D)))
        for h in heads:
            hand_over(d_copy, dmap, dsend, h)

    halo_copy(1).wait_recv()

    @pl.loop(0, HK)
    def _(kh):
        arrived(1, kh)
        vn = conv_silu(1, wv, kh).astype(BF)
        vs[kh] = vn
        for j in range(2):
            h = 2 * kh + j
            asend[h] = nn(mb[h], vn[:, j * D : (j + 1) * D]).astype(BF)
        for j in range(2):
            hand_over(a_copy, amap, asend, 2 * kh + j)

    halo_copy(2).wait_recv()

    def own_tokens(pair):
        for kh in (2 * pair, 2 * pair + 1):
            arrived(2, kh)
        qn = [unit(conv_silu(2, wq, kh), D ** -0.5) for kh in (2 * pair, 2 * pair + 1)]
        todo = []
        for g in range(2):
            kh = 2 * pair + g
            kn = ks[kh]
            qk00, qk1 = nt(qn[g][:D], kn[:D]), nt(qn[g][D:], kn)
            for j in range(2):
                h = 2 * kh + j
                todo.append((kh, j, h, g, dec[h, 0] * qk00, dec[h, 1] * qk1[:, :D], dec[h, 2] * qk1[:, D:]))
        m1 = [hi + nn(hi.astype(BF), tmat[h, 1]) for _, _, h, _, _, _, hi in todo]
        m0 = [lo - nn(x.astype(BF), nmat[h, 1]) for x, (_, _, h, _, _, lo, _) in zip(m1, todo)]
        p00 = [top + nn(top.astype(BF), tmat[h, 0]) for _, _, h, _, top, _, _ in todo]
        m0 = [x + nn(x.astype(BF), tmat[h, 0]) for x, (_, _, h, _, _, _, _) in zip(m0, todo)]
        for n, (kh, j, h, g, _, _, _) in enumerate(todo):
            grow = jnp.exp(ccol[kh][:, j : j + 1])
            bt = brow[h]
            btg = bt * jnp.exp(crow[h])
            kn, vj, qf = ks[kh], vs[kh][:, j * D : (j + 1) * D], qn[g].astype(F32)
            p1 = jnp.concatenate([m0[n], m1[n]], axis=1)
            o0[h, pl.ds(0, D), :] = nn((p00[n] * bt[:, :D]).astype(BF), vj[:D])
            o0[h, pl.ds(D, D), :] = nn((p1 * bt).astype(BF), vj)
            gmat[h, pl.ds(0, D), :] = (grow[:D] * qf[:D] - nn((p00[n] * btg[:, :D]).astype(BF), kn[:D])).astype(BF)
            gmat[h, pl.ds(D, D), :] = (grow[D:] * qf[D:] - nn((p1 * btg).astype(BF), kn)).astype(BF)

    own_tokens(0)

    def wait_from(copy, i):
        @pl.when(mine != i)
        def _():
            copy(i, i).wait_recv()

    for i in range(GRP):
        wait_from(d_copy, i)
    lin = [dmap[i, pl.ds(0, D), :] for i in range(GRP)]
    decays = [load_exact(dmap.at[i]) for i in range(GRP)]
    xd, ep = lin[0].astype(F32), decays[0]
    sd, es = lin[GRP - 1].astype(F32), decays[GRP - 1]
    pxd[0] = jnp.zeros((D, D), BF)
    pep[0] = jnp.ones((1, D), F32)
    for i in range(1, GRP):
        xb = xd.astype(BF)
        pxd[i] = xb
        pep[i] = ep
        xd = decays[i] * xd + nn(lin[i], xb) + ep * lin[i].astype(F32)
        ep = ep * decays[i]
        m = GRP - 1 - i
        sb = sd.astype(BF)
        sfx[:, m * D : (m + 1) * D] = sb
        sfe[m] = es
        if m > 0:
            sd = decays[m] * sd + nn(sb, lin[m]) + es * lin[m].astype(F32)
            es = es * decays[m]
    gds[pl.ds(0, D), :] = xd.astype(BF)
    store_exact(gds, ep)

    def yd_copy(d):
        return remote(gds, gdm.at[yrow], yd_s.at[d - 1], yd_r.at[yrow], {"ctx": lax.rem(ctx + d * GRP, nctx)})

    def ya_copy(d):
        return remote(gas, gam.at[yrow], ya_s.at[d - 1], ya_r.at[yrow], {"ctx": lax.rem(ctx + d * GRP, nctx)})

    for d in range(1, 4):
        @pl.when((yrow > 0) & (yrow + d < nrow))
        def _():
            yd_copy(d).start()

    for i in range(GRP):
        wait_from(a_copy, i)
    add = [amap[i] for i in range(GRP)]
    total = add[GRP - 1].astype(F32) + nn(sfx[...], jnp.concatenate(add[: GRP - 1], axis=0))
    for i in range(GRP - 1):
        total = total + sfe[i] * add[i].astype(F32)
    gas[...] = total.astype(BF)
    for d in range(1, 4):
        @pl.when(yrow + d < nrow)
        def _():
            ya_copy(d).start()

    xa = add[0].astype(F32)
    pxa[0] = jnp.zeros((D, D), F32)
    for i in range(1, GRP):
        pxa[i] = xa
        if i < GRP - 1:
            xa = decays[i] * xa + nn(lin[i], xa.astype(BF)) + add[i].astype(F32)
    own_tokens(1)

    state[...] = jnp.zeros_like(state)
    for yy in range(3):
        @pl.when(yy < yrow)
        def _():
            remote(gas, gam.at[yy], ya_s.at[0], ya_r.at[yy], {"ctx": prev}).wait_recv()
            if yy == 0:
                state[...] = gam[0].astype(F32)
            else:
                remote(gds, gdm.at[yy], yd_s.at[0], yd_r.at[yy], {"ctx": prev}).wait_recv()
                s_now = state[...]
                state[...] = (
                    load_exact(gdm.at[yy]) * s_now
                    + nn(gdm[yy, pl.ds(0, D), :], s_now.astype(BF))
                    + gam[yy].astype(F32)
                )

    def state_copy(i, slot):
        return remote(ssend.at[i], sbuf.at[my_head], st_s.at[i], st_r.at[slot], {"ctx": base + i})

    s_in = state[...]
    moved = nn(jnp.concatenate([pxd[i] for i in range(GRP)], axis=0), s_in.astype(BF))
    for i in range(GRP):
        ssend[i] = (pep[i] * s_in + moved[i * D : (i + 1) * D] + pxa[i]).astype(BF)
    for t in range(1, GRP):
        state_copy(lax.rem(mine + t, GRP), my_head).start()
    sbuf[my_head] = ssend[mine]

    def ret_copy(d, h, slot):
        return remote(
            nb.at[pl.ds(aligned(peer(d) * BLK, BLK), BLK), pl.ds(aligned(h * D, D), D)],
            out.at[:, pl.ds(aligned(me * HV * D + h * D, D), D)],
            ret_s.at[h, d - 1], ret_r.at[h, slot], {"head": peer(d)},
        )

    @pl.loop(0, GRP)
    def _(t):
        h = head_of(lax.rem(mine + GRP - t, GRP))

        @pl.when(t > 0)
        def _():
            state_copy(h, h).wait_recv()

        core = o0[h] + nn(gmat[h], sbuf[h])
        inv = lax.rsqrt(jnp.mean(core * core, axis=-1, keepdims=True) + 1e-6)
        nb[:, pl.ds(aligned(h * D, D), D)] = (core * inv * wgain[...]).astype(BF)
        for d in (2, 1, 3):
            ret_copy(d, h, d - 1).start()

    own_out = pltpu.make_async_copy(
        nb.at[my_rows, :], out.at[:, pl.ds(aligned(me * HV * D, HV * D), HV * D)], loc.at[0]
    )
    own_out.start()
    for d in (1, 3, 2):
        @pl.loop(0, HV)
        def _(h):
            ret_copy(d, h, d - 1).wait_recv()
    own_out.wait()

    for d in range(1, NH):
        for i in range(2):
            ab_copy(d, i).wait_send()

        @pl.loop(0, HK)
        def _(kh):
            for i in range(3):
                rows_copy(i, d, kh).wait_send()

        @pl.loop(0, HV)
        def _(h):
            ret_copy(d, h, d - 1).wait_send()

        @pl.when(yrow + d < nrow)
        def _():
            ya_copy(d).wait_send()

        @pl.when((yrow > 0) & (yrow + d < nrow))
        def _():
            yd_copy(d).wait_send()

    for i in range(3):
        halo_copy(i).wait_send()

    @pl.when(me == NH - 1)
    def _():
        for i in range(3):
            for d in range(1, NH):
                tail_copy(i, d).wait_send()

    @pl.loop(0, GRP)
    def _(i):
        @pl.when(i != my_head)
        def _():
            d_copy(i, mine).wait_send()
            a_copy(i, mine).wait_send()

        @pl.when(i != mine)
        def _():
            state_copy(i, my_head).wait_send()


def local(q, k, v, z, a, b, cq, ck, cv, alog, dtb, gain):
    any_spec = pl.BlockSpec(memory_space=pl.ANY)
    dma = pltpu.SemaphoreType.DMA

    def bf(*shape):
        return pltpu.VMEM(shape, BF)

    def f32(*shape):
        return pltpu.VMEM(shape, F32)

    scratch = dict(
        rq=bf(C, 512), rk=bf(C, 512), rv=bf(C, 1024), ra=bf(NH, 32, BLK), rb=bf(NH, 32, BLK),
        hq=bf(RIM, 512), hk=bf(RIM, 512), hv=bf(RIM, 1024), tq=bf(RIM, 512), tk=bf(RIM, 512), tv=bf(RIM, 1024), xs=f32(C + RIM, 256),
        wq=f32(4, 512), wk=f32(4, 512), wv=f32(4, 1024), walog=f32(1, HV), wdtb=f32(1, HV), wgain=f32(1, D),
        masks=bf(8, D, D), ccol=f32(HK, C, 4), crow=f32(HV, 1, C), brow=f32(HV, 1, C),
        dec=f32(HV, 3, D, D), nmat=bf(HV, 3, D, D), tmat=bf(HV, 2, D, D), ks=bf(HK, C, D), vs=bf(HK, C, 2 * D),
        kdt=bf(HV, D, C), mb=bf(HV, D, C), o0=f32(HV, C, D), gmat=bf(HV, C, D),
        dsend=bf(HV, D + 16, D), asend=bf(HV, D, D), dmap=bf(GRP, D + 16, D), amap=bf(GRP, D, D),
        pxd=bf(GRP, D, D), pxa=f32(GRP, D, D), pep=f32(GRP, 1, D), sfx=bf(D, (GRP - 1) * D), sfe=f32(GRP, 1, D),
        gds=bf(D + 16, D), gas=bf(D, D), gdm=bf(4, D + 16, D), gam=bf(4, D, D),
        state=f32(D, D), ssend=bf(GRP, D, D), sbuf=bf(HV, D, D), nb=bf(C, HV * D),
        k_s=dma((HK, 3)), k_r=dma((HK, 3)), v_s=dma((HK, 3)), v_r=dma((HK, 3)), q_s=dma((HK, 3)), q_r=dma((HK, 3)),
        ab_s=dma((3, 2)), ab_r=dma((3, 2)), tail_s=dma((3, 3)), tail_r=dma((3,)),
        halo_s=dma((3,)), halo_r=dma((3,)), loc=dma((11,)),
        d_s=dma((GRP,)), d_r=dma((GRP,)), a_s=dma((GRP,)), a_r=dma((GRP,)),
        yd_s=dma((3,)), yd_r=dma((4,)), ya_s=dma((3,)), ya_r=dma((4,)),
        st_s=dma((GRP,)), st_r=dma((GRP,)), ret_s=dma((HV, 3)), ret_r=dma((HV, 3)),
    )
    normed = pl.pallas_call(
        kernel,
        out_shape=pltpu.VMEM((BLK, 4 * HV * D), BF),
        in_specs=[any_spec] * 11,
        out_specs=any_spec,
        scratch_shapes=list(scratch.values()),
        compiler_params=pltpu.CompilerParams(
            collective_id=0, has_side_effects=True, vmem_limit_bytes=60 * 1024 * 1024
        ),
    )(q, k, v, a.T, b.T, cq, ck, cv, alog.reshape(1, HV), dtb.reshape(1, HV), gain.reshape(1, D))
    return (normed.astype(F32) * jax.nn.silu(z.astype(F32))).astype(BF)


def solution(mesh):
    rows = P(("ctx", "head"), None)
    placed = (rows,) * 6 + (P(None, "head"),) * 3 + (P("head"), P("head"), P())
    return jax.shard_map(local, mesh=mesh, in_specs=placed, out_specs=rows, check_vma=False)
```
